128 devices in a mesh: blk: 8 (over y, core), expert: 16 (over x, z).
Axes of the slice: x: 4, y: 4, z: 4, core: 2. Of those that a mesh axis runs over, the one named last changes fastest.
Arguments:
- prefill_rows: bfloat16 [16384, 2048], P(('blk', 'expert')), may hold values from -6 to 6
- decode_rows: bfloat16 [4, 2048], replicated, may hold values from -6 to 6
- key_values: bfloat16 [2, 4, 16384, 2048], P(None, None, 'blk', 'expert')
- cache_length: int32 [4], replicated, may hold values from 1 to 16384, as said below
- attention_gain: float32 [2048], replicated, may hold values from 0.25 to 1.75
- feedforward_gain: float32 [2048], replicated, may hold values from 0.25 to 1.75
- query_key_value: bfloat16 [2048, 3, 2048], P(None, None, 'expert')
- out_projection: bfloat16 [2048, 2048], P('expert'), may hold values from -0.125 to 0.125
- routes: int32 [16384, 4], P(('blk', 'expert')), may hold values from 0 to 15, all different within a row; in each aligned block of 128 rows (0 to 127, 128 to 255, ...) at most 48 rows name the same one
- route_weight: float32 [16384, 4], P(('blk', 'expert')), may hold values from 0.1 to 0.6
- decode_routes: int32 [4, 4], replicated, may hold values from 0 to 15, as said below
- decode_weight: float32 [4, 4], replicated, may hold values from 0.5 to 1
- expert_gate_up: bfloat16 [16, 2048, 2816], P('expert'), may hold values from -0.125 to 0.125
- expert_down: bfloat16 [16, 1408, 2048], P('expert'), may hold values from -0.15625 to 0.15625
- shared_gate_up: bfloat16 [2048, 2, 5632], P(None, None, 'expert'), may hold values from -0.125 to 0.125
- shared_down: bfloat16 [5632, 2048], P('expert'), may hold values from -0.078125 to 0.078125
- shared_gate: float32 [2048], replicated, may hold values from -0.25 to 0.25
Outputs:
- prefill_out: bfloat16 [16384, 2048], P(('blk', 'expert'))
- decode_out: bfloat16 [4, 2048], replicated
The draws below stay inside these ranges and needn't reach their ends.
Inputs may be any that keep to these rules, and one draw needn't show every extreme that they name: `routes`: each row names 4 different experts; among the rows of one device no expert is named more than 48 times, and some expert reaches that count. Request d's cache is valid at its first cache_length[d] positions; one request fills all 16384. `decode_routes`: each row names 4 different experts; every expert is named by some row.
All inputs are finite; a program needn't handle non-finite values.
Results may differ from the reference program's by a relative error of at most 0.02.
Values may be sent and summed in bfloat16 or wider, within the bound.
A program may use at most 128 MiB of HBM per device.

```python
import math
import jax
import jax.numpy as jnp
import numpy as np
from jax import lax

D = 2048
HEADS = 16
HEAD_DIM = 128
EXPERT_FF = 1408
SHARED_FF = 5632
TOP_K = 4
REQUEST_LEN = 1024
PREFILL_DEV = 128
DECODE = 4
CACHE_DEV = 2048
EXPERTS = 16
CAPACITY = 48
CACHE = 16384
TOKENS = 16384
N_BLK = 8
N_EXPERT = 16


def draw_key_values(key, part):
    normal_noise = jax.random.normal(jax.random.fold_in(key, 11), (2, DECODE, CACHE, HEADS * HEAD_DIM), jnp.float32)
    offsets = 2.0 * jax.random.normal(jax.random.fold_in(key, 12), (DECODE, CACHE // CACHE_DEV, HEADS * HEAD_DIM), jnp.float32)
    region = jnp.repeat(offsets, CACHE_DEV, axis=1)
    key_part = normal_noise[0]
    value_part = normal_noise[1] + region
    return jnp.stack([key_part, value_part]).astype(jnp.bfloat16)


def draw_query_key_value(key, part):
    weights = jax.random.normal(jax.random.fold_in(key, 21), (D, 3, HEADS * HEAD_DIM), jnp.float32) / math.sqrt(D)
    return weights.astype(jnp.bfloat16)


def draw_cache_length(key, part):
    length_key, full_key = jax.random.split(jax.random.fold_in(key, 31))
    lengths = jax.random.randint(length_key, (DECODE,), 1, CACHE + 1)
    fullest = jax.random.randint(full_key, (), 0, DECODE)
    return jnp.where(jnp.arange(DECODE) == fullest, CACHE, lengths).astype(jnp.int32)


def draw_decode_routes(key, part):
    order = jax.random.permutation(jax.random.fold_in(key, 41), EXPERTS)
    place = (jnp.arange(DECODE)[:, None] * TOP_K + jnp.arange(TOP_K)[None, :]) % EXPERTS
    return order[place].astype(jnp.int32)


def levels(own_key, extent, shards, smallest, high):
    factor_of = 1.0
    for axis_at, shards_of in shards:
        heights = jax.random.uniform(jax.random.fold_in(jax.random.fold_in(own_key, 6), axis_at), (shards_of,), jnp.float32, smallest / len(shards), high / len(shards))
        factor_of = factor_of * jnp.repeat(jnp.exp(heights), extent[axis_at] // shards_of).reshape((-1,) + (1,) * (len(extent) - 1 - axis_at))
    return factor_of


def deal_out(own_key, own, number, rows, number_of, top, limit, skew):
    sequence = jax.random.permutation(own_key, number_of)
    heavy_load, common = load_shares(number_of, rows * top, limit, skew, True), load_shares(number_of, rows * top, limit, skew, False)
    places = jnp.arange(number_of)

    def named(sizes, turn):
        used = int((sizes > 0).sum())
        fixed = max(1, used // 4)
        moved = fixed + (places - fixed + turn * (used - fixed)) % max(1, number_of - fixed)
        return jnp.zeros((number_of,), jnp.int32).at[sequence[jnp.where(places < fixed, places, moved)]].set(jnp.asarray(sizes, jnp.int32))

    sizes = jnp.where(number % 4 == 0, named(heavy_load, number // 4), named(common, number - number // 4 - 1))
    mixed = jax.random.permutation(jax.random.fold_in(own, 3), number_of)
    giver, taker = mixed[0:number_of // 2 * 2:2], mixed[1:number_of // 2 * 2:2]
    margin = jnp.minimum(sizes[giver] - 1, limit - sizes[taker]) // 2
    margin = jnp.where((giver == sequence[0]) | (taker == sequence[0]) | (sizes[taker] == 0), 0, jnp.maximum(margin, 0))
    moved = jax.random.randint(jax.random.fold_in(own, 4), (number_of // 2,), 0, 1 << 20) % (margin + 1)
    sizes = sizes.at[giver].add(-moved).at[taker].add(moved)
    members = jnp.searchsorted(jnp.cumsum(sizes), jnp.arange(rows * top), side="right").astype(jnp.int32)
    grid = members.reshape(top, rows).T
    grid = grid[jax.random.permutation(jax.random.fold_in(own, 1), rows)]
    turn = jax.random.randint(jax.random.fold_in(own, 2), (rows, 1), 0, top)
    return jnp.take_along_axis(grid, (jnp.arange(top)[None, :] + turn) % top, axis=1)


def load_shares(amount, total, reach, slope, full):
    weights = [(1 << 20) // math.isqrt(grade ** slope) + 1 for grade in range(1, amount + 1)]
    largest = reach if full else min(reach, max(-(-total // amount), total * weights[0] // sum(weights)))
    least = 1 if total - largest >= amount - 1 else 0
    given, surplus = [largest] + [least] * (amount - 1), total - largest - least * (amount - 1)
    while surplus > 0:
        free = [i for i in range(1, amount) if given[i] < largest] or [i for i in range(1, amount) if given[i] < reach]
        mass, remaining = sum([weights[i] for i in free]), surplus
        for i in free:
            addition = min(reach - given[i], max(1, remaining * weights[i] // mass), surplus)
            given[i] = given[i] + addition
            surplus = surplus - addition
    return np.array(given)


def noise(rng, dims, spread, limit, pieces=(), kind=jnp.bfloat16):
    values = jax.random.normal(rng, dims, jnp.float32) * spread
    if len(pieces) > 0:
        values = levels(rng, dims, pieces, -0.22, 0.18) * values
    return jnp.clip(values, min=-limit, max=limit).astype(kind)


def setup_inputs(seed: int = 0) -> dict:
    arg_keys = jax.random.split(jax.random.key(seed), 18)
    prefill_rows = noise(arg_keys[0], (TOKENS, D), 1.0, 6.0, ((0, 128),))
    decode_rows = noise(arg_keys[1], (DECODE, D), 1.0, 6.0)
    key_values = draw_key_values(jax.random.fold_in(arg_keys[17], 71), 0)
    cache_length = draw_cache_length(jax.random.fold_in(arg_keys[17], 71), 0)
    attention_gain = jnp.clip(1.0 + 0.15 * jax.random.normal(arg_keys[4], (D,), jnp.float32), 0.25, 1.75)
    feedforward_gain = jnp.clip(1.0 + 0.15 * jax.random.normal(arg_keys[5], (D,), jnp.float32), 0.25, 1.75)
    query_key_value = draw_query_key_value(jax.random.fold_in(arg_keys[17], 71), 0)
    out_projection = noise(arg_keys[7], (HEADS * HEAD_DIM, D), (HEADS * HEAD_DIM) ** -0.5, 0.125, ((0, 16),))
    routes_keys = jax.random.split(jax.random.fold_in(arg_keys[8], 1), TOKENS // PREFILL_DEV)
    routes_turns = jax.random.permutation(jax.random.fold_in(arg_keys[8], 3), TOKENS // PREFILL_DEV)
    routes = jax.vmap(lambda own, number: deal_out(jax.random.fold_in(arg_keys[8], 2), own, number, PREFILL_DEV, EXPERTS, TOP_K, CAPACITY, 2))(routes_keys, routes_turns).reshape((TOKENS, TOP_K))
    route_weight = jnp.clip(0.1 + 0.5 * jax.random.uniform(arg_keys[9], (TOKENS, TOP_K), jnp.float32) ** levels(arg_keys[9], (TOKENS, TOP_K), ((0, 128),), -0.2, 0.2), 0.1, 0.6)
    decode_routes = draw_decode_routes(jax.random.fold_in(arg_keys[17], 71), 0)
    decode_weight = jnp.clip(jax.random.uniform(arg_keys[11], (DECODE, TOP_K), jnp.float32, 0.5, 1.0), 0.5, 1.0)
    expert_gate_up = noise(arg_keys[12], (EXPERTS, D, 2 * EXPERT_FF), D ** -0.5, 0.125, ((0, 16),))
    expert_down = noise(arg_keys[13], (EXPERTS, EXPERT_FF, D), EXPERT_FF ** -0.5, 0.15625, ((0, 16),))
    shared_gate_up = noise(arg_keys[14], (D, 2, SHARED_FF), D ** -0.5, 0.125, ((2, 16),))
    shared_down = noise(arg_keys[15], (SHARED_FF, D), SHARED_FF ** -0.5, 0.078125, ((0, 16),))
    shared_gate = noise(arg_keys[16], (D,), (D // 4) ** -0.5, 0.25, (), jnp.float32)
    return dict(prefill_rows=prefill_rows, decode_rows=decode_rows, key_values=key_values, cache_length=cache_length, attention_gain=attention_gain, feedforward_gain=feedforward_gain, query_key_value=query_key_value, out_projection=out_projection, routes=routes, route_weight=route_weight, decode_routes=decode_routes, decode_weight=decode_weight, expert_gate_up=expert_gate_up, expert_down=expert_down, shared_gate_up=shared_gate_up, shared_down=shared_down, shared_gate=shared_gate)


eps_norm = 1e-06

def rms_normed(matrix, gain_vector):
    values = matrix.astype(jnp.float32)
    factor = lax.rsqrt(lax.optimization_barrier(jnp.mean(values * values, axis=-1, keepdims=True)) + eps_norm)
    return (values * factor * gain_vector).astype(jnp.bfloat16)

def gated_hidden(normed, gate_up):
    hidden = jnp.dot(normed, gate_up, preferred_element_type=jnp.float32)
    half_width = hidden.shape[1] // 2
    return (jax.nn.silu(hidden[:, :half_width]) * hidden[:, half_width:]).astype(jnp.bfloat16)

def grouped_sum(left, right, groups):
    inner = left.shape[1] // groups
    left_parts = jnp.transpose(left.reshape(left.shape[0], groups, inner), (1, 0, 2))
    right_parts = right.reshape(groups, inner, right.shape[1])

    def add_group(carry, pair):
        term = jnp.dot(pair[0], pair[1], preferred_element_type=jnp.float32)
        rounded = lax.optimization_barrier(term.astype(jnp.bfloat16))
        return (carry + rounded.astype(jnp.float32), None)
    start_sum = jnp.zeros((left.shape[0], right.shape[1]), jnp.float32)
    return lax.scan(add_group, start_sum, (left_parts, right_parts))[0]

def request_attention(request_block):
    score_scale = 1.0 / math.sqrt(HEAD_DIM)
    query_block = request_block[:, 0].astype(jnp.float32)
    key_block = request_block[:, 1].astype(jnp.float32)
    value_block = request_block[:, 2].astype(jnp.float32)
    position = jnp.arange(REQUEST_LEN)
    causal = position[:, None] >= position[None, :]
    scores = jnp.einsum('qhc,khc->hqk', query_block, key_block) * score_scale
    scores = jnp.where(causal[None], scores, -jnp.inf)
    weights = jnp.exp(scores - lax.optimization_barrier(jnp.max(scores, axis=-1, keepdims=True)))
    probabilities = (weights / lax.optimization_barrier(jnp.sum(weights, axis=-1, keepdims=True))).astype(jnp.bfloat16)
    mixture = jnp.einsum('hqk,khc->qhc', probabilities.astype(jnp.float32), value_block)
    return mixture.astype(jnp.bfloat16)

def reference(prefill_rows, decode_rows, key_values, cache_length, attention_gain, feedforward_gain, query_key_value, out_projection, routes, route_weight, decode_routes, decode_weight, expert_gate_up, expert_down, shared_gate_up, shared_down, shared_gate):
    group_rows = PREFILL_DEV * N_EXPERT
    projection = query_key_value.reshape(D, 3 * HEADS * HEAD_DIM)
    shared_matrix = shared_gate_up.reshape(D, 2 * SHARED_FF)
    expert_ids = jnp.arange(EXPERTS, dtype=jnp.int32)

    def feed_forward(normed, residual, route_ids, route_scale, most_rows):
        activated = gated_hidden(normed, shared_matrix)
        shared_sum = grouped_sum(activated, shared_down, N_EXPERT)
        gate_value = jax.nn.sigmoid(lax.optimization_barrier(jnp.sum(normed.astype(jnp.float32) * shared_gate, axis=-1)))

        def add_expert(carry, expert_item):
            expert, gate_up, down_matrix = expert_item
            matches = route_ids == expert
            row_scale = lax.optimization_barrier(jnp.sum(jnp.where(matches, route_scale, 0.0), axis=1))
            chosen = jnp.any(matches, axis=1)
            picked = jnp.nonzero(chosen, size=most_rows, fill_value=0)[0].astype(jnp.int32)
            is_live = jnp.arange(most_rows) < jnp.sum(chosen.astype(jnp.int32))
            output = jnp.dot(gated_hidden(normed[picked], gate_up), down_matrix, preferred_element_type=jnp.float32).astype(jnp.bfloat16)
            update = jnp.where(is_live, row_scale[picked], 0.0)[:, None] * output.astype(jnp.float32)
            return (carry.at[picked].add(update), None)
        routed = lax.scan(add_expert, jnp.zeros(residual.shape, jnp.float32), (expert_ids, expert_gate_up, expert_down))[0]
        return (residual.astype(jnp.float32) + gate_value[:, None] * shared_sum + routed).astype(jnp.bfloat16)

    def prefill_group(group):
        rows_in, route_ids, route_scale = group
        normed = rms_normed(rows_in, attention_gain)
        projected = jnp.dot(normed, projection, preferred_element_type=jnp.float32).astype(jnp.bfloat16)
        blocks = projected.reshape(group_rows // REQUEST_LEN, REQUEST_LEN, 3, HEADS, HEAD_DIM)
        attended = lax.map(request_attention, blocks).reshape(group_rows, HEADS * HEAD_DIM)
        head_sum = grouped_sum(attended, out_projection, N_EXPERT)
        residual = (rows_in.astype(jnp.float32) + head_sum).astype(jnp.bfloat16)
        return feed_forward(rms_normed(residual, feedforward_gain), residual, route_ids, route_scale, N_EXPERT * CAPACITY)
    prefill_out = lax.map(prefill_group, (prefill_rows.reshape(N_BLK, group_rows, D), routes.reshape(N_BLK, group_rows, TOP_K), route_weight.reshape(N_BLK, group_rows, TOP_K))).reshape(TOKENS, D)
    decode_normed = rms_normed(decode_rows, attention_gain)
    decode_projected = jnp.dot(decode_normed, projection, preferred_element_type=jnp.float32).astype(jnp.bfloat16)
    decode_projected = decode_projected.reshape(DECODE, 3, HEADS, HEAD_DIM)

    def decode_request(request):
        query_row, key_new, value_new, cache_keys, cache_values, length = request
        score_scale = 1.0 / math.sqrt(HEAD_DIM)
        query_wide = query_row.astype(jnp.float32)
        key_matrix = cache_keys.reshape(CACHE, HEADS, HEAD_DIM).astype(jnp.float32)
        value_matrix = cache_values.reshape(CACHE, HEADS, HEAD_DIM).astype(jnp.float32)
        scores = jnp.einsum('hc,phc->hp', query_wide, key_matrix, precision=lax.Precision.HIGHEST) * score_scale
        valid = (jnp.arange(CACHE) < length)[None, :]
        masked = jnp.where(valid, scores, -1e+30)
        new_score = lax.optimization_barrier(jnp.sum(query_wide * key_new.astype(jnp.float32), axis=-1)) * score_scale
        top_score = jnp.maximum(lax.optimization_barrier(jnp.max(masked, axis=-1)), new_score)
        weights = jnp.where(valid, jnp.exp(masked - top_score[:, None]), 0.0)
        new_weight = jnp.exp(new_score - top_score)
        denominator = lax.optimization_barrier(jnp.sum(weights, axis=-1)) + new_weight
        mixture = jnp.einsum('hp,phc->hc', weights, value_matrix, precision=lax.Precision.HIGHEST) + new_weight[:, None] * value_new.astype(jnp.float32)
        return (mixture / denominator[:, None]).astype(jnp.bfloat16).reshape(HEADS * HEAD_DIM)
    decode_attended = lax.map(decode_request, (decode_projected[:, 0], decode_projected[:, 1], decode_projected[:, 2], key_values[0], key_values[1], cache_length))
    decode_head = grouped_sum(decode_attended, out_projection, N_EXPERT)
    decode_residual = (decode_rows.astype(jnp.float32) + decode_head).astype(jnp.bfloat16)
    decode_out = feed_forward(rms_normed(decode_residual, feedforward_gain), decode_residual, decode_routes, decode_weight, DECODE)
    return (prefill_out, decode_out)
```

```python
import math

import jax
import jax.numpy as jnp
from jax import lax
from jax.experimental import pallas as pl
from jax.experimental.pallas import tpu as pltpu
from jax.sharding import PartitionSpec as P

HEAD_DIM = 128
REQUEST_LEN = 1024
EPS = 1e-06
MESH = pl.DeviceIdType.MESH
F32 = jnp.float32
BF16 = jnp.bfloat16

BATCHES = (
    ((0, 0), (0, 1), (0, 3), (1, 0), (3, 0)),
    ((1, 1), (1, 3), (3, 1), (3, 3), (2, 0), (0, 2)),
    ((1, 2), (3, 2), (2, 1), (2, 3), (2, 2)),
)
SLOT = {place: at for at, place in enumerate(sum(BATCHES, ()))}
STARTS = (0, 5, 11)


def nn(a, b):
    return lax.dot_general(a, b, (((1,), (0,)), ((), ())), preferred_element_type=F32)


def nt(a, b):
    return lax.dot_general(a, b, (((1,), (1,)), ((), ())), preferred_element_type=F32)


def normed(values, gain):
    factor = lax.rsqrt(jnp.mean(values * values, axis=-1, keepdims=True) + EPS)
    return (values * factor * gain).astype(BF16)


def silu(v):
    return v * (1.0 / (1.0 + jnp.exp(-v)))


class Place:
    def __init__(self):
        self.b = lax.axis_index("blk")
        self.e = lax.axis_index("expert")
        self.x = self.e // 4
        self.z = self.e % 4

    def at(self, dx, dz):
        return (self.b, ((self.x + dx) % 4) * 4 + (self.z + dz) % 4)

    def block(self, place):
        return ((self.x + place[0]) % 4) * 4 + (self.z + place[1]) % 4


def greet(peers):
    barrier = pltpu.get_barrier_semaphore()
    for peer in peers:
        pl.semaphore_signal(barrier, inc=1, device_id=peer, device_id_type=MESH)
    return lambda: pl.semaphore_wait(barrier, len(peers))


def remote(src, dst, send, recv, at, device):
    return pltpu.make_async_remote_copy(
        src_ref=src,
        dst_ref=dst,
        send_sem=send.at[at],
        recv_sem=recv.at[at],
        device_id=device,
        device_id_type=MESH,
    )


def slot(half, p, q):
    return SLOT[(p, q) if half == 0 else (q, p)]


def sides(here, half):
    along_x = (here.at(1, 0), here.at(3, 0))
    along_z = (here.at(0, 1), here.at(0, 3))
    return along_x + along_z if half == 0 else along_z + along_x


class Gather:
    def __init__(self, here, rows_ref, rows, send, recv, base):
        self.copies = []
        hr = rows // 2
        for half in range(2):
            major_p, major_m, minor_p, minor_m = sides(here, half)
            c = {}

            def put(name, at, src, dst, part, device):
                lo, size = part
                c[name] = remote(
                    rows_ref.at[half, pl.ds(slot(half, *src) * rows + lo, size)],
                    rows_ref.at[half, pl.ds(slot(half, *dst) * rows + lo, size)],
                    send,
                    recv,
                    base + half * 20 + at,
                    device,
                )

            whole, low, high = (0, rows), (0, hr), (hr, hr)
            put("n+", 0, (0, 0), (0, 3), whole, minor_p)
            put("n-", 1, (0, 0), (0, 1), whole, minor_m)
            put("fn+", 4, (0, 3), (0, 2), high, minor_p)
            put("fn-", 5, (0, 1), (0, 2), low, minor_m)
            for q, at in ((0, 2), (1, 6), (3, 8), (2, 10)):
                put(("j+", q), at, (0, q), (3, q), whole, major_p)
                put(("j-", q), at + 1, (0, q), (1, q), whole, major_m)
            for q, at in ((0, 12), (1, 14), (3, 16), (2, 18)):
                put(("f+", q), at, (3, q), (2, q), high, major_p)
                put(("f-", q), at + 1, (1, q), (2, q), low, major_m)
            self.copies.append(c)

    def start(self, *names):
        for c in self.copies:
            for name in names:
                c[name].start()

    def got(self, *names):
        for c in self.copies:
            for name in names:
                c[name].wait_recv()

    def open(self):
        self.start("n+", "n-", ("j+", 0), ("j-", 0))

    def to_batch_0(self):
        self.got("n+", "n-")
        self.start("fn+", "fn-", ("j+", 1), ("j-", 1), ("j+", 3), ("j-", 3))
        self.got(("j+", 0), ("j-", 0))
        self.start(("f+", 0), ("f-", 0))

    def to_batch_1(self):
        self.got("fn+", "fn-")
        self.start(("j+", 2), ("j-", 2))
        self.got(("j+", 1), ("j-", 1))
        self.start(("f+", 1), ("f-", 1))
        self.got(("j+", 3), ("j-", 3))
        self.start(("f+", 3), ("f-", 3))
        self.got(("f+", 0), ("f-", 0))

    def to_batch_2(self):
        self.got(("j+", 2), ("j-", 2))
        self.start(("f+", 2), ("f-", 2))
        for q in (1, 3, 2):
            self.got(("f+", q), ("f-", q))

    def close(self):
        for c in self.copies:
            for copy in c.values():
                copy.wait_send()


class Scatter:
    def __init__(self, here, part_ref, fwd_ref, full_ref, send, recv, base):
        self.part, self.fwd, self.full = part_ref, fwd_ref, full_ref
        self.copies = []
        rows = part_ref.shape[2]
        hr = rows // 2
        self.low, self.high = pl.ds(0, hr), pl.ds(hr, hr)
        for half in range(2):
            major_p, major_m, minor_p, minor_m = sides(here, half)
            c = {}

            def put(q, far, plus, minus, side_p, side_m):
                at = base + half * 20 + 4 * q
                c["f+", q] = remote(
                    part_ref.at[half, far, self.low], fwd_ref.at[half, q, 0], send, recv, at, side_p
                )
                c["f-", q] = remote(
                    part_ref.at[half, far, self.high], fwd_ref.at[half, q, 1], send, recv, at + 1, side_m
                )
                c["t+", q] = remote(
                    part_ref.at[half, plus], full_ref.at[half, q, 0], send, recv, at + 2, side_p
                )
                c["t-", q] = remote(
                    part_ref.at[half, minus], full_ref.at[half, q, 1], send, recv, at + 3, side_m
                )

            for q in range(4):
                put(q, slot(half, 2, q), slot(half, 1, q), slot(half, 3, q), major_p, major_m)
            put(4, slot(half, 0, 2), slot(half, 0, 1), slot(half, 0, 3), minor_p, minor_m)
            self.copies.append(c)

    def _next(self, half, q, p):
        return slot(half, p, q) if q < 4 else slot(half, 0, p)

    def send_far(self, *qs):
        for q in qs:
            for half in range(2):
                self.copies[half]["f+", q].start()
                self.copies[half]["f-", q].start()

    def pass_plus(self, half, q):
        c = self.copies[half]
        c["f+", q].wait_recv()
        at = self._next(half, q, 1)
        self.part[half, at, self.low] = (
            self.part[half, at, self.low].astype(F32) + self.fwd[half, q, 0].astype(F32)
        ).astype(BF16)
        c["t+", q].start()

    def pass_minus(self, half, q):
        c = self.copies[half]
        c["f-", q].wait_recv()
        at = self._next(half, q, 3)
        self.part[half, at, self.high] = (
            self.part[half, at, self.high].astype(F32) + self.fwd[half, q, 1].astype(F32)
        ).astype(BF16)
        c["t-", q].start()

    def pass_on(self, *qs):
        for q in qs:
            for half in range(2):
                self.pass_plus(half, q)
                self.pass_minus(half, q)

    def total(self, half, q):
        c = self.copies[half]
        c["t+", q].wait_recv()
        c["t-", q].wait_recv()
        at = self._next(half, q, 0)
        return (
            self.part[half, at].astype(F32)
            + self.full[half, q, 0].astype(F32)
            + self.full[half, q, 1].astype(F32)
        )

    def line(self, q):
        for half in range(2):
            self.part[half, slot(half, 0, q)] = self.total(half, q).astype(BF16)

    def finish(self):
        self.line(2)
        self.send_far(4)
        self.line(1)
        for half in range(2):
            self.pass_plus(half, 4)
        self.line(3)
        for half in range(2):
            self.pass_minus(half, 4)
        self.line(0)
        return [self.total(half, 4) for half in range(2)]

    def close(self):
        for c in self.copies:
            for copy in c.values():
                copy.wait_send()


def padded_rows(ref, scratch):
    scratch[...] = jnp.zeros_like(scratch)
    scratch[0 : ref.shape[0], :] = ref[...].astype(F32)
    return scratch[...]


def attention_kernel(
    rows_ref,
    dec_ref,
    cache_hbm,
    length_ref,
    gain_ref,
    qkv_hbm,
    att_ref,
    dec_att_ref,
    g,
    wqkv,
    cache,
    heads,
    dec8,
    dec_out,
    dec_in,
    send,
    recv,
    local_sem,
):
    here = Place()
    rows, width = rows_ref.shape
    hw = width // 2
    blk_count = lax.axis_size("blk")
    score_scale = 1.0 / math.sqrt(HEAD_DIM)
    w_copy = pltpu.make_async_copy(qkv_hbm, wqkv, local_sem.at[0])
    c_copy = pltpu.make_async_copy(cache_hbm, cache, local_sem.at[1])
    w_copy.start()
    c_copy.start()
    core, y = here.b % 2, here.b // 2
    blk_peers = []
    if blk_count > 1:
        blk_peers = [(here.b + 1 - 2 * core, here.e)]
        blk_peers += [(((y + k) % 4) * 2 + core, here.e) for k in (1, 3, 2)]
    wait_all = greet([here.at(1, 0), here.at(3, 0), here.at(0, 1), here.at(0, 3)] + blk_peers)
    own = normed(rows_ref[...].astype(F32), gain_ref[...])
    g[0, 0:rows] = own[:, :hw]
    g[1, 0:rows] = own[:, hw:]
    wait_all()
    gather = Gather(here, g, rows, send, recv, 0)
    gather.open()

    dn = normed(padded_rows(dec_ref, dec8), gain_ref[...])
    w_copy.wait()
    q8 = nn(dn, wqkv[0]).astype(BF16)
    k8 = nn(dn, wqkv[1]).astype(BF16)
    v8 = nn(dn, wqkv[2]).astype(BF16)
    c_copy.wait()
    count = cache.shape[1]
    span = cache.shape[2]
    row = lax.broadcasted_iota(jnp.int32, (8, 1), 0)
    scores = jnp.zeros((8, span), F32)
    lengths = jnp.zeros((8, 1), jnp.int32)
    for d in range(count):
        scores = jnp.where(row == d, nt(q8, cache[0, d]), scores)
        lengths = jnp.where(row == d, length_ref[d], lengths)
    position = here.b * span + lax.broadcasted_iota(jnp.int32, (8, span), 1)
    valid = position < lengths
    masked = jnp.where(valid, scores * score_scale, -1e30)
    top = jnp.max(masked, axis=-1, keepdims=True)
    weights = jnp.where(valid, jnp.exp(masked - top), 0.0)
    total = jnp.sum(weights, axis=-1, keepdims=True)
    coarse = weights.astype(BF16).astype(F32)
    both = jnp.concatenate([coarse, weights - coarse], axis=0).astype(BF16)
    mix = jnp.zeros((8, HEAD_DIM), F32)
    for d in range(count):
        pair = nn(both, cache[1, d])
        mix = jnp.where(row == d, pair[0:8] + pair[8:16], mix)

    def pack(at, mix, top, total):
        dec_out[at, 0:8] = mix
        dec_out[at, 8:16] = jnp.broadcast_to(top, (8, HEAD_DIM))
        dec_out[at, 16:24] = jnp.broadcast_to(total, (8, HEAD_DIM))

    def merge(mix, top, total, at):
        other_top = dec_in[at, 8:16]
        new_top = jnp.maximum(top, other_top)
        mine, theirs = jnp.exp(top - new_top), jnp.exp(other_top - new_top)
        return (
            mix * mine + dec_in[at, 0:8] * theirs,
            new_top,
            total * mine + dec_in[at, 16:24] * theirs,
        )

    top = jnp.broadcast_to(top, (8, HEAD_DIM))
    total = jnp.broadcast_to(total, (8, HEAD_DIM))
    pack(0, mix, top, total)
    blk_copies = [
        remote(dec_out.at[min(k, 1)], dec_in.at[k], send, recv, 40 + k, peer)
        for k, peer in enumerate(blk_peers)
    ]
    for copy in blk_copies[:1]:
        copy.start()

    q_s, k_s, v_s = heads.at[0], heads.at[1], heads.at[2]

    def project(batch):
        lo, size = STARTS[batch] * rows, len(BATCHES[batch]) * rows
        left, right = g[0, lo : lo + size], g[1, lo : lo + size]
        for which, ref in enumerate((q_s, k_s, v_s)):
            out = (nn(left, wqkv[which, 0:hw]) + nn(right, wqkv[which, hw:width])).astype(BF16)
            for j, place in enumerate(BATCHES[batch]):
                at = pl.multiple_of(here.block(place) * rows, rows)
                ref[pl.ds(at, rows)] = out[j * rows : (j + 1) * rows]

    gather.to_batch_0()
    project(0)
    gather.to_batch_1()
    if blk_copies:
        blk_copies[0].wait_recv()
        mix, top, total = merge(mix, top, total, 0)
        pack(1, mix, top, total)
        for copy in blk_copies[1:]:
            copy.start()
    project(1)
    gather.to_batch_2()
    project(2)
    for k, copy in enumerate(blk_copies[1:]):
        copy.wait_recv()
        mix, top, total = merge(mix, top, total, k + 1)
    q32, k32, v32 = q8.astype(F32), k8.astype(F32), v8.astype(F32)
    new_score = jnp.sum(q32 * k32, axis=-1, keepdims=True) * score_scale
    new_top = jnp.maximum(top, new_score)
    old = jnp.exp(top - new_top)
    fresh = jnp.exp(new_score - new_top)
    dec_att_ref[...] = ((mix * old + fresh * v32) / (total * old + fresh)).astype(BF16)

    step = 256
    diagonal = lax.broadcasted_iota(jnp.int32, (step, step), 0) >= lax.broadcasted_iota(
        jnp.int32, (step, step), 1
    )

    def one_request(r, carry):
        first = pl.multiple_of(r * REQUEST_LEN, REQUEST_LEN)
        for qb in range(REQUEST_LEN // step):
            at = pl.multiple_of(first + qb * step, step)
            q = q_s[pl.ds(at, step)]
            s1 = jnp.where(diagonal, nt(q, k_s[pl.ds(at, step)]) * score_scale, -jnp.inf)
            top_q = jnp.max(s1, axis=-1, keepdims=True)
            if qb:
                s0 = nt(q, k_s[pl.ds(first, qb * step)]) * score_scale
                top_q = jnp.maximum(top_q, jnp.max(s0, axis=-1, keepdims=True))
            p1 = jnp.exp(s1 - top_q)
            sum_q = jnp.sum(p1, axis=-1, keepdims=True)
            out = nn(p1.astype(BF16), v_s[pl.ds(at, step)])
            if qb:
                p0 = jnp.exp(s0 - top_q)
                sum_q = sum_q + jnp.sum(p0, axis=-1, keepdims=True)
                out = out + nn(p0.astype(BF16), v_s[pl.ds(first, qb * step)])
            att_ref[pl.ds(at, step)] = (out / sum_q).astype(BF16)
        return carry

    lax.fori_loop(0, att_ref.shape[0] // REQUEST_LEN, one_request, 0)
    gather.close()
    for copy in blk_copies:
        copy.wait_send()


def layer_kernel(
    rows_ref,
    dec_ref,
    att_ref,
    dec_att_ref,
    gain_ref,
    wo_ref,
    routes_ref,
    weight_ref,
    dec_routes_ref,
    dec_weight_ref,
    gate_ref,
    wgu_hbm,
    wd_hbm,
    wst_hbm,
    wsd_hbm,
    out_ref,
    dec_out_ref,
    g,
    part,
    fwd,
    full,
    wgu,
    wd,
    wsp,
    wsd,
    xe,
    he,
    ye,
    hs,
    gv,
    wslot,
    pick,
    back,
    meta,
    dec8,
    dec_send,
    dec_recv,
    res,
    send,
    recv,
    local_sem,
):
    here = Place()
    rows, width = rows_ref.shape
    hw = width // 2
    cap = pick.shape[1]
    ff = wd.shape[0]
    sff = wsd_hbm.shape[0]
    count = dec_ref.shape[0]
    tail = sff - 256
    tile = min(256, hw)

    moves = [(wgu_hbm, wgu), (wd_hbm, wd), (wsd_hbm, wsd.at[pl.ds(0, sff)])]
    for group, size in enumerate((128, 128, tail)):
        for kind in range(2):
            moves.append(
                (
                    wst_hbm.at[kind, pl.ds(group * 128, size)],
                    wsp.at[pl.ds(group * 256 + kind * 128, size)],
                )
            )
    local = [pltpu.make_async_copy(a, b, local_sem.at[i]) for i, (a, b) in enumerate(moves)]
    for copy in local:
        copy.start()
    peers = [here.at(1, 0), here.at(3, 0), here.at(0, 1), here.at(0, 3), here.at(2, 0), here.at(0, 2)]
    wait_all = greet(peers)

    weight = weight_ref[...]
    coarse = weight.astype(BF16).astype(F32)
    meta[0, 0] = jnp.concatenate(
        [routes_ref[...].astype(F32), coarse, weight - coarse, jnp.zeros_like(weight)], axis=0
    ).astype(BF16)

    def out_project(*places):
        for place in places:
            at = pl.multiple_of(here.block(place) * rows, rows)
            term = nn(att_ref[pl.ds(at, rows)], wo_ref[...]).astype(BF16)
            part[0, SLOT[place]] = term[:, :hw]
            part[1, SLOT[place]] = term[:, hw:]

    first = Scatter(here, part, fwd, full, send, recv, 0)
    gather = Gather(here, g, rows, send, recv, 40)
    second = Scatter(here, part, fwd, full, send, recv, 80)

    def exchange(buf_send, buf_recv, base, along):
        steps = ((1, 0), (3, 0), (2, 0)) if along == 0 else ((0, 1), (0, 3), (0, 2))
        return [
            remote(buf_send, buf_recv.at[k], send, recv, base + k, here.at(*step))
            for k, step in enumerate(steps)
        ]

    meta_z = [
        remote(meta.at[0, 0], meta.at[0, dst], send, recv, 120 + k, here.at(0, dz))
        for k, (dz, dst) in enumerate(((1, 3), (3, 1), (2, 2)))
    ]
    meta_x = [
        remote(meta.at[0], meta.at[dst], send, recv, 123 + k, here.at(dx, 0))
        for k, (dx, dst) in enumerate(((1, 3), (3, 1), (2, 2)))
    ]
    dec_copies = [
        exchange(dec_send.at[k], dec_recv.at[k], 126 + 3 * k, 1 - k % 2) for k in range(4)
    ]

    out_project((2, 2))
    dec_term = nn(dec_att_ref[...], wo_ref[...])
    dec_send[0] = dec_term.astype(BF16)
    wait_all()
    first.send_far(2)
    for copy in meta_z + dec_copies[0]:
        copy.start()
    out_project((2, 1), (1, 2))
    first.send_far(1)
    out_project((2, 3), (3, 2))
    first.send_far(3)
    out_project((2, 0), (0, 2))
    first.send_far(0)
    out_project((1, 1), (3, 1), (1, 3), (3, 3))
    first.pass_on(2)
    out_project((1, 0), (3, 0), (0, 1), (0, 3), (0, 0))
    first.pass_on(1)

    def dec_sum(k):
        total = dec_send[k].astype(F32)
        for copy in dec_copies[k]:
            copy.wait_recv()
        for at in range(3):
            total = total + dec_recv[k, at].astype(F32)
        return total

    for copy in meta_z:
        copy.wait_recv()
    for copy in meta_x:
        copy.start()
    dec_send[1] = dec_sum(0).astype(BF16)
    for copy in dec_copies[1]:
        copy.start()
    first.pass_on(3, 0)

    gate = gate_ref[...]
    gate_coarse = gate.astype(BF16).astype(F32)
    for copy in local:
        copy.wait()
    pad = 128 - tail
    row_at = lax.broadcasted_iota(jnp.int32, (pad, width), 0)
    wsp[512 + tail : 640] = jnp.where(
        row_at == 0, gate_coarse, jnp.where(row_at == 1, gate - gate_coarse, 0.0)
    ).astype(BF16)
    wsp[640 + tail : 768] = jnp.zeros((pad, width), BF16)
    wsd[sff : wsd.shape[0]] = jnp.zeros((wsd.shape[0] - sff, width), BF16)

    for copy in meta_x:
        copy.wait_recv()
    expert = here.e.astype(F32)
    iota_r = lax.broadcasted_iota(jnp.int32, (rows, rows), 0)
    iota_c = lax.broadcasted_iota(jnp.int32, (rows, rows), 1)
    upper = (iota_r <= iota_c).astype(F32).astype(BF16)
    eye = (iota_r == iota_c).astype(F32).astype(BF16)
    iota_cap = lax.broadcasted_iota(jnp.int32, (cap, rows), 0).astype(F32)
    iota_lane = iota_c.astype(F32)
    for place, at in SLOT.items():
        info = meta[place[0], place[1]].astype(F32)
        match = info[0:4] == expert
        chosen = jnp.sum(match.astype(F32), axis=0, keepdims=True)
        scale = jnp.sum(jnp.where(match, info[4:8] + info[8:12], 0.0), axis=0, keepdims=True)
        order = nn(jnp.broadcast_to(chosen, (8, rows)).astype(BF16), upper)[0:1] - 1.0
        order = jnp.where(chosen > 0.0, order, -1.0)
        choice = iota_cap == order
        pick[at] = choice.astype(F32).astype(BF16)
        wslot[at] = jnp.broadcast_to(
            jnp.sum(jnp.where(choice, scale, 0.0), axis=1, keepdims=True), (cap, 128)
        )
        column = nt(eye, jnp.broadcast_to(order, (8, rows)).astype(BF16))[:, 0:1]
        back[at] = (iota_lane == column).astype(F32).astype(BF16)

    dec_res = (padded_rows(dec_ref, dec8) + dec_sum(1)).astype(BF16).astype(F32)
    dec_two = normed(dec_res, gain_ref[...])
    dec8[...] = dec_res
    base_row = 16 * rows
    dec_pad = jnp.concatenate([dec_two.astype(F32), jnp.zeros((8, width), F32)], axis=0).astype(BF16)
    g[0, base_row : base_row + 16] = dec_pad[:, :hw]
    g[1, base_row : base_row + 16] = dec_pad[:, hw:]

    halves = first.finish()
    sum_sq = jnp.zeros((rows, 1), F32)
    for half in range(2):
        cols = pl.ds(half * hw, hw)
        value = (rows_ref[:, cols].astype(F32) + halves[half]).astype(BF16)
        res[:, cols] = value
        wide = value.astype(F32)
        sum_sq = sum_sq + jnp.sum(wide * wide, axis=-1, keepdims=True)
    factor = lax.rsqrt(sum_sq / width + EPS)
    for half in range(2):
        cols = pl.ds(half * hw, hw)
        g[half, 0:rows] = (res[:, cols].astype(F32) * factor * gain_ref[:, cols]).astype(BF16)
    gather.open()
    first.close()

    row8 = lax.broadcasted_iota(jnp.int32, (16, 1), 0)
    dec_scale = jnp.zeros((16, 1), F32)
    for d in range(count):
        one = jnp.float32(0.0)
        for k in range(dec_routes_ref.shape[1]):
            one = one + jnp.where(dec_routes_ref[d, k] == here.e, dec_weight_ref[d, k], 0.0)
        dec_scale = jnp.where(row8 == d, one, dec_scale)

    def feed_forward(batch):
        places = BATCHES[batch]
        start, n = STARTS[batch], len(places)
        decode = batch == 2
        extra = 16 if decode else 0
        m, me = n * rows + extra, n * cap + extra
        lo = start * rows
        for j in range(n):
            at = lo + j * rows
            for half in range(2):
                xe[j * cap : (j + 1) * cap, half * hw : (half + 1) * hw] = nn(
                    pick[start + j], g[half, at : at + rows]
                ).astype(BF16)
        if decode:
            xe[n * cap : me] = dec_pad

        def up(i, carry):
            at = pl.multiple_of(i * 128, 128)
            w = jnp.concatenate([wgu[:, pl.ds(at, 128)], wgu[:, pl.ds(ff + at, 128)]], axis=1)
            hidden = nn(xe[0:me], w)
            he[0:me, pl.ds(at, 128)] = (silu(hidden[:, 0:128]) * hidden[:, 128:256]).astype(BF16)
            return carry

        lax.fori_loop(0, ff // 128, up, 0)

        scale = jnp.concatenate(
            [wslot[start + j][:, 0:1] for j in range(n)] + ([dec_scale] if decode else []), axis=0
        )

        def down(i, carry):
            cols = pl.ds(pl.multiple_of(i * tile, tile), tile)
            ye[0:me, cols] = (nn(he[0:me], wd[:, cols]) * scale).astype(BF16)
            return carry

        lax.fori_loop(0, width // tile, down, 0)

        for group in range(3):
            w = wsp.at[pl.ds(group * 256, 256)]
            hidden = nt(g[0, lo : lo + m], w[:, 0:hw]) + nt(g[1, lo : lo + m], w[:, hw:width])
            hs[0:m, group * 128 : (group + 1) * 128] = (
                silu(hidden[:, 0:128]) * hidden[:, 128:256]
            ).astype(BF16)
            if group == 2:
                logit = hidden[:, tail : tail + 1] + hidden[:, tail + 1 : tail + 2]
                gv[0:m] = jnp.broadcast_to(1.0 / (1.0 + jnp.exp(-logit)), (m, 128))

        for half in range(2):

            def combine(i, carry, half=half):
                here_cols = pl.ds(pl.multiple_of(i * tile, tile), tile)
                cols = pl.ds(pl.multiple_of(half * hw + i * tile, tile), tile)
                shared = nn(hs[0:m], wsd[:, cols]) * gv[0:m, 0:1]
                for j in range(n):
                    routed = nn(back[start + j][:, 0:cap], ye[j * cap : (j + 1) * cap, cols])
                    part[half, start + j, :, here_cols] = (
                        shared[j * rows : (j + 1) * rows] + routed
                    ).astype(BF16)
                if decode:
                    dec_send[2, :, cols] = (
                        shared[n * rows : n * rows + 8] + ye[n * cap : n * cap + 16, cols].astype(F32)[0:8]
                    ).astype(BF16)
                return carry

            lax.fori_loop(0, hw // tile, combine, 0)

    gather.to_batch_0()
    feed_forward(0)
    gather.to_batch_1()
    feed_forward(1)
    second.send_far(0)
    gather.to_batch_2()
    second.pass_on(0)
    feed_forward(2)
    second.send_far(2, 1, 3)
    for copy in dec_copies[2]:
        copy.start()
    second.pass_on(2, 1, 3)
    dec_send[3] = dec_sum(2).astype(BF16)
    for copy in dec_copies[3]:
        copy.start()
    halves = second.finish()
    for half in range(2):
        cols = pl.ds(half * hw, hw)
        out_ref[:, cols] = (res[:, cols].astype(F32) + halves[half]).astype(BF16)
    dec_out_ref[...] = (dec8[...] + dec_sum(3)).astype(BF16)[0:count]
    gather.close()
    second.close()
    for copy in meta_z + meta_x + sum(dec_copies, []):
        copy.wait_send()


def per_device(
    prefill_rows,
    decode_rows,
    key_values,
    cache_length,
    attention_gain,
    feedforward_gain,
    query_key_value,
    out_projection,
    routes,
    route_weight,
    decode_routes,
    decode_weight,
    expert_gate_up,
    expert_down,
    shared_gate_up,
    shared_down,
    shared_gate,
):
    rows, width = prefill_rows.shape
    hw = width // 2
    tokens = rows * 16
    count, span = decode_rows.shape[0], key_values.shape[2]
    cap = 3 * rows * routes.shape[1] // 32
    ff = expert_down.shape[1]
    vmem = pl.BlockSpec(memory_space=pltpu.VMEM)
    smem = pl.BlockSpec(memory_space=pltpu.SMEM)
    hbm = pl.BlockSpec(memory_space=pl.ANY)
    most = max(len(b) for b in BATCHES)
    attended, decode_attended = pl.pallas_call(
        attention_kernel,
        out_shape=(
            jax.ShapeDtypeStruct((tokens, HEAD_DIM), BF16),
            jax.ShapeDtypeStruct((8, HEAD_DIM), BF16),
        ),
        in_specs=[vmem, vmem, hbm, smem, vmem, hbm],
        out_specs=(vmem, vmem),
        scratch_shapes=[
            pltpu.VMEM((2, tokens, hw), BF16),
            pltpu.VMEM((3, width, HEAD_DIM), BF16),
            pltpu.VMEM((2, count, span, HEAD_DIM), BF16),
            pltpu.VMEM((3, tokens, HEAD_DIM), BF16),
            pltpu.VMEM((8, width), F32),
            pltpu.VMEM((2, 24, HEAD_DIM), F32),
            pltpu.VMEM((4, 24, HEAD_DIM), F32),
            pltpu.SemaphoreType.DMA((44,)),
            pltpu.SemaphoreType.DMA((44,)),
            pltpu.SemaphoreType.DMA((2,)),
        ],
        compiler_params=pltpu.CompilerParams(
            collective_id=0, has_side_effects=True, vmem_limit_bytes=48 * 1024 * 1024
        ),
        name="attend",
    )(
        prefill_rows,
        decode_rows,
        key_values,
        cache_length,
        attention_gain.reshape(1, width),
        jnp.transpose(query_key_value, (1, 0, 2)),
    )
    return pl.pallas_call(
        layer_kernel,
        out_shape=(
            jax.ShapeDtypeStruct((rows, width), BF16),
            jax.ShapeDtypeStruct((count, width), BF16),
        ),
        in_specs=[vmem] * 8 + [smem] * 2 + [vmem] + [hbm] * 4,
        out_specs=(vmem, vmem),
        scratch_shapes=[
            pltpu.VMEM((2, tokens + 16, hw), BF16),
            pltpu.VMEM((2, 16, rows, hw), BF16),
            pltpu.VMEM((2, 5, 2, rows // 2, hw), BF16),
            pltpu.VMEM((2, 5, 2, rows, hw), BF16),
            pltpu.VMEM((width, 2 * ff), BF16),
            pltpu.VMEM((ff, width), BF16),
            pltpu.VMEM((768, width), BF16),
            pltpu.VMEM((384, width), BF16),
            pltpu.VMEM((most * cap + 16, width), BF16),
            pltpu.VMEM((most * cap + 16, ff), BF16),
            pltpu.VMEM((most * cap + 16, width), BF16),
            pltpu.VMEM((most * rows + 16, 384), BF16),
            pltpu.VMEM((most * rows + 16, 128), F32),
            pltpu.VMEM((16, cap, 128), F32),
            pltpu.VMEM((16, cap, rows), BF16),
            pltpu.VMEM((16, rows, rows), BF16),
            pltpu.VMEM((4, 4, 16, rows), BF16),
            pltpu.VMEM((8, width), F32),
            pltpu.VMEM((4, 8, width), BF16),
            pltpu.VMEM((4, 3, 8, width), BF16),
            pltpu.VMEM((rows, width), BF16),
            pltpu.SemaphoreType.DMA((138,)),
            pltpu.SemaphoreType.DMA((138,)),
            pltpu.SemaphoreType.DMA((9,)),
        ],
        compiler_params=pltpu.CompilerParams(
            collective_id=1, has_side_effects=True, vmem_limit_bytes=67043328
        ),
        name="layer",
    )(
        prefill_rows,
        decode_rows,
        attended,
        decode_attended,
        feedforward_gain.reshape(1, width),
        out_projection,
        routes.T,
        route_weight.T,
        decode_routes,
        decode_weight,
        shared_gate.reshape(1, width),
        expert_gate_up[0],
        expert_down[0],
        jnp.transpose(shared_gate_up, (1, 2, 0)),
        shared_down,
    )


def solution(mesh):
    return jax.shard_map(
        per_device,
        mesh=mesh,
        in_specs=(
            P(("blk", "expert"), None),
            P(),
            P(None, None, "blk", "expert"),
            P(),
            P(),
            P(),
            P(None, None, "expert"),
            P("expert", None),
            P(("blk", "expert"), None),
            P(("blk", "expert"), None),
            P(),
            P(),
            P("expert", None, None),
            P("expert", None, None),
            P(None, None, "expert"),
            P("expert", None),
            P(),
        ),
        out_specs=(P(("blk", "expert"), None), P()),
        check_vma=False,
    )
```

```python
import math

import jax
import jax.numpy as jnp
from jax import lax
from jax.experimental import pallas as pl
from jax.experimental.pallas import tpu as pltpu
from jax.sharding import PartitionSpec as P

HEAD_DIM = 128
REQUEST_LEN = 1024
EPS = 1e-06
MESH = pl.DeviceIdType.MESH
F32 = jnp.float32
BF16 = jnp.bfloat16

BATCHES = (
    ((0, 0), (0, 1), (0, 3), (1, 0), (3, 0)),
    ((1, 1), (1, 3), (3, 1), (3, 3), (2, 0), (0, 2)),
    ((1, 2), (3, 2), (2, 1), (2, 3), (2, 2)),
)
SLOT = {place: at for at, place in enumerate(sum(BATCHES, ()))}
STARTS = (0, 5, 11)
PAIR_BATCHES = (((0, 0), (0, 1), (0, 3), (1, 0)), ((0, 2), (1, 1), (1, 3), (1, 2)))
PAIR = {place: at for at, place in enumerate(sum(PAIR_BATCHES, ()))}


def nn(a, b):
    return lax.dot_general(a, b, (((1,), (0,)), ((), ())), preferred_element_type=F32)


def nt(a, b):
    return lax.dot_general(a, b, (((1,), (1,)), ((), ())), preferred_element_type=F32)


def normed(values, gain):
    factor = lax.rsqrt(jnp.mean(values * values, axis=-1, keepdims=True) + EPS)
    return (values * factor * gain).astype(BF16)


def silu(v):
    return v * (1.0 / (1.0 + jnp.exp(-v)))


class Place:
    def __init__(self):
        self.b = lax.axis_index("blk")
        self.e = lax.axis_index("expert")
        self.x = self.e // 4
        self.z = self.e % 4

        odd = self.x % 2
        self.mate = lambda: self.at(1 + 2 * odd, 0)
        self.other = lambda: self.at(3 - 2 * odd, 0)
        self.odd = odd

    def at(self, dx, dz):
        return (self.b, ((self.x + dx) % 4) * 4 + (self.z + dz) % 4)

    def block(self, place):
        half = self.odd if place[0] == 0 else 1 - self.odd
        return half * 4 + (self.z + place[1]) % 4


def greet(peers):
    barrier = pltpu.get_barrier_semaphore()
    for peer in peers:
        pl.semaphore_signal(barrier, inc=1, device_id=peer, device_id_type=MESH)
    return lambda: pl.semaphore_wait(barrier, len(peers))


def remote(src, dst, send, recv, at, device):
    return pltpu.make_async_remote_copy(
        src_ref=src,
        dst_ref=dst,
        send_sem=send.at[at],
        recv_sem=recv.at[at],
        device_id=device,
        device_id_type=MESH,
    )


def slot(half, p, q):
    return SLOT[(p, q) if half == 0 else (q, p)]


def sides(here, half):
    along_x = (here.at(1, 0), here.at(3, 0))
    along_z = (here.at(0, 1), here.at(0, 3))
    return along_x + along_z if half == 0 else along_z + along_x


class Gather:
    def __init__(self, here, rows_ref, rows, send, recv, base):
        self.copies = []
        hr = rows // 2
        for half in range(2):
            major_p, major_m, minor_p, minor_m = sides(here, half)
            c = {}

            def put(name, at, src, dst, part, device):
                lo, size = part
                c[name] = remote(
                    rows_ref.at[half, pl.ds(slot(half, *src) * rows + lo, size)],
                    rows_ref.at[half, pl.ds(slot(half, *dst) * rows + lo, size)],
                    send,
                    recv,
                    base + half * 20 + at,
                    device,
                )

            whole, low, high = (0, rows), (0, hr), (hr, hr)
            put("n+", 0, (0, 0), (0, 3), whole, minor_p)
            put("n-", 1, (0, 0), (0, 1), whole, minor_m)
            put("fn+", 4, (0, 3), (0, 2), high, minor_p)
            put("fn-", 5, (0, 1), (0, 2), low, minor_m)
            for q, at in ((0, 2), (1, 6), (3, 8), (2, 10)):
                put(("j+", q), at, (0, q), (3, q), whole, major_p)
                put(("j-", q), at + 1, (0, q), (1, q), whole, major_m)
            for q, at in ((0, 12), (1, 14), (3, 16), (2, 18)):
                put(("f+", q), at, (3, q), (2, q), high, major_p)
                put(("f-", q), at + 1, (1, q), (2, q), low, major_m)
            self.copies.append(c)

    def start(self, *names):
        for c in self.copies:
            for name in names:
                c[name].start()

    def got(self, *names):
        for c in self.copies:
            for name in names:
                c[name].wait_recv()

    def open(self):
        self.start("n+", "n-", ("j+", 0), ("j-", 0))

    def to_batch_0(self):
        self.got("n+", "n-")
        self.start("fn+", "fn-", ("j+", 1), ("j-", 1), ("j+", 3), ("j-", 3))
        self.got(("j+", 0), ("j-", 0))
        self.start(("f+", 0), ("f-", 0))

    def to_batch_1(self):
        self.got("fn+", "fn-")
        self.start(("j+", 2), ("j-", 2))
        self.got(("j+", 1), ("j-", 1))
        self.start(("f+", 1), ("f-", 1))
        self.got(("j+", 3), ("j-", 3))
        self.start(("f+", 3), ("f-", 3))
        self.got(("f+", 0), ("f-", 0))

    def to_batch_2(self):
        self.got(("j+", 2), ("j-", 2))
        self.start(("f+", 2), ("f-", 2))
        for q in (1, 3, 2):
            self.got(("f+", q), ("f-", q))

    def close(self):
        for c in self.copies:
            for copy in c.values():
                copy.wait_send()


class PairGather:
    def __init__(self, here, rows_ref, rows, send, recv):
        hr = rows // 2
        self.c = c = {}
        z_p, z_m, mate = here.at(0, 1), here.at(0, 3), here.mate()

        def put(name, half, src, dst, lo, size, device):
            c[name] = remote(
                rows_ref.at[half, pl.ds(PAIR[src] * rows + lo, size)],
                rows_ref.at[half, pl.ds(PAIR[dst] * rows + lo, size)],
                send,
                recv,
                len(c),
                device,
            )

        for half, a in ((0, 0), (1, 0), (1, 1)):
            put(("+", half, a), half, (a, 0), (a, 3), 0, rows, z_p)
            put(("-", half, a), half, (a, 0), (a, 1), 0, rows, z_m)
            put(("f+", half, a), half, (a, 3), (a, 2), hr, hr, z_p)
            put(("f-", half, a), half, (a, 1), (a, 2), 0, hr, z_m)
        for q in (0, 1, 3, 2):
            put(("m", 0, q), 0, (0, q), (1, q), 0, rows, mate)
        put(("m", 1, 0), 1, (0, 0), (1, 0), 0, rows, mate)

    def start(self, *names):
        for name in names:
            self.c[name].start()

    def got(self, *names):
        for name in names:
            self.c[name].wait_recv()

    def open(self):
        self.start(("+", 0, 0), ("-", 0, 0), ("m", 1, 0), ("m", 0, 0), ("+", 1, 0), ("-", 1, 0))

    def to_batch_0(self):
        self.got(("+", 0, 0), ("-", 0, 0))
        self.start(("f+", 0, 0), ("f-", 0, 0), ("m", 0, 1), ("m", 0, 3))
        self.got(("m", 1, 0))
        self.start(("+", 1, 1), ("-", 1, 1))
        self.got(("+", 1, 0), ("-", 1, 0))
        self.start(("f+", 1, 0), ("f-", 1, 0))
        self.got(("m", 0, 0))

    def relay(self):
        self.got(("f+", 0, 0), ("f-", 0, 0))
        self.start(("m", 0, 2))
        self.got(("+", 1, 1), ("-", 1, 1))
        self.start(("f+", 1, 1), ("f-", 1, 1))

    def to_batch_1(self):
        self.got(("m", 0, 1), ("m", 0, 3), ("m", 0, 2))
        self.got(("f+", 1, 0), ("f-", 1, 0), ("f+", 1, 1), ("f-", 1, 1))

    def close(self):
        for copy in self.c.values():
            copy.wait_send()


class PairScatter:
    def __init__(self, here, part_ref, fwd_ref, full_ref, send, recv):
        self.part, self.fwd, self.full = part_ref, fwd_ref, full_ref
        self.c = c = {}
        rows = part_ref.shape[2]
        hr = rows // 2
        self.low, self.high = pl.ds(0, hr), pl.ds(hr, hr)
        z_p, z_m, mate = here.at(0, 1), here.at(0, 3), here.mate()

        def put(name, src, dst, device):
            c[name] = remote(src, dst, send, recv, len(c), device)

        for half, a, k in ((0, 0, 4), (1, 1, 1), (1, 0, 0)):
            far, plus, minus = PAIR[a, 2], PAIR[a, 1], PAIR[a, 3]
            put(("f+", half, a), part_ref.at[half, far, self.low], fwd_ref.at[half, k, 0], z_p)
            put(("f-", half, a), part_ref.at[half, far, self.high], fwd_ref.at[half, k, 1], z_m)
            put(("t+", half, a), part_ref.at[half, plus], full_ref.at[half, k, 0], z_p)
            put(("t-", half, a), part_ref.at[half, minus], full_ref.at[half, k, 1], z_m)
        for q in range(4):
            put(("m", 0, q), part_ref.at[0, PAIR[1, q]], full_ref.at[0, q, 0], mate)
        put(("m", 1, 0), part_ref.at[1, PAIR[1, 0]], full_ref.at[1, 4, 0], mate)
        self.slots = {(0, 0): 4, (1, 1): 1, (1, 0): 0}

    def start(self, *names):
        for name in names:
            self.c[name].start()

    def far(self, half, a):
        self.start(("f+", half, a), ("f-", half, a))

    def pass_plus(self, half, a):
        self.c["f+", half, a].wait_recv()
        at, k = PAIR[a, 1], self.slots[half, a]
        self.part[half, at, self.low] = (
            self.part[half, at, self.low].astype(F32) + self.fwd[half, k, 0].astype(F32)
        ).astype(BF16)
        self.c["t+", half, a].start()

    def pass_minus(self, half, a):
        self.c["f-", half, a].wait_recv()
        at, k = PAIR[a, 3], self.slots[half, a]
        self.part[half, at, self.high] = (
            self.part[half, at, self.high].astype(F32) + self.fwd[half, k, 1].astype(F32)
        ).astype(BF16)
        self.c["t-", half, a].start()

    def ring(self, half, a):
        self.c["t+", half, a].wait_recv()
        self.c["t-", half, a].wait_recv()
        k = self.slots[half, a]
        return (
            self.part[half, PAIR[a, 0]].astype(F32)
            + self.full[half, k, 0].astype(F32)
            + self.full[half, k, 1].astype(F32)
        )

    def meet(self, q):
        self.c["m", 0, q].wait_recv()
        at = PAIR[0, q]
        self.part[0, at] = (self.part[0, at].astype(F32) + self.full[0, q, 0].astype(F32)).astype(BF16)

    def finish(self):
        self.meet(2)
        self.far(0, 0)
        self.meet(1)
        self.pass_plus(0, 0)
        self.meet(3)
        self.pass_minus(0, 0)
        self.part[1, PAIR[1, 0]] = self.ring(1, 1).astype(BF16)
        self.start(("m", 1, 0))
        self.meet(0)
        right = self.ring(1, 0)
        left = self.ring(0, 0)
        self.c["m", 1, 0].wait_recv()
        return [left, right + self.full[1, 4, 0].astype(F32)]

    def close(self):
        for copy in self.c.values():
            copy.wait_send()


class Scatter:
    def __init__(self, here, part_ref, fwd_ref, full_ref, send, recv, base):
        self.part, self.fwd, self.full = part_ref, fwd_ref, full_ref
        self.copies = []
        rows = part_ref.shape[2]
        hr = rows // 2
        self.low, self.high = pl.ds(0, hr), pl.ds(hr, hr)
        for half in range(2):
            major_p, major_m, minor_p, minor_m = sides(here, half)
            c = {}

            def put(q, far, plus, minus, side_p, side_m):
                at = base + half * 20 + 4 * q
                c["f+", q] = remote(
                    part_ref.at[half, far, self.low], fwd_ref.at[half, q, 0], send, recv, at, side_p
                )
                c["f-", q] = remote(
                    part_ref.at[half, far, self.high], fwd_ref.at[half, q, 1], send, recv, at + 1, side_m
                )
                c["t+", q] = remote(
                    part_ref.at[half, plus], full_ref.at[half, q, 0], send, recv, at + 2, side_p
                )
                c["t-", q] = remote(
                    part_ref.at[half, minus], full_ref.at[half, q, 1], send, recv, at + 3, side_m
                )

            for q in range(4):
                put(q, slot(half, 2, q), slot(half, 1, q), slot(half, 3, q), major_p, major_m)
            put(4, slot(half, 0, 2), slot(half, 0, 1), slot(half, 0, 3), minor_p, minor_m)
            self.copies.append(c)

    def _next(self, half, q, p):
        return slot(half, p, q) if q < 4 else slot(half, 0, p)

    def send_far(self, *qs):
        for q in qs:
            for half in range(2):
                self.copies[half]["f+", q].start()
                self.copies[half]["f-", q].start()

    def pass_plus(self, half, q):
        c = self.copies[half]
        c["f+", q].wait_recv()
        at = self._next(half, q, 1)
        self.part[half, at, self.low] = (
            self.part[half, at, self.low].astype(F32) + self.fwd[half, q, 0].astype(F32)
        ).astype(BF16)
        c["t+", q].start()

    def pass_minus(self, half, q):
        c = self.copies[half]
        c["f-", q].wait_recv()
        at = self._next(half, q, 3)
        self.part[half, at, self.high] = (
            self.part[half, at, self.high].astype(F32) + self.fwd[half, q, 1].astype(F32)
        ).astype(BF16)
        c["t-", q].start()

    def pass_on(self, *qs):
        for q in qs:
            for half in range(2):
                self.pass_plus(half, q)
                self.pass_minus(half, q)

    def total(self, half, q):
        c = self.copies[half]
        c["t+", q].wait_recv()
        c["t-", q].wait_recv()
        at = self._next(half, q, 0)
        return (
            self.part[half, at].astype(F32)
            + self.full[half, q, 0].astype(F32)
            + self.full[half, q, 1].astype(F32)
        )

    def line(self, q):
        for half in range(2):
            self.part[half, slot(half, 0, q)] = self.total(half, q).astype(BF16)

    def finish(self):
        self.line(2)
        self.send_far(4)
        self.line(1)
        for half in range(2):
            self.pass_plus(half, 4)
        self.line(3)
        for half in range(2):
            self.pass_minus(half, 4)
        self.line(0)
        return [self.total(half, 4) for half in range(2)]

    def close(self):
        for c in self.copies:
            for copy in c.values():
                copy.wait_send()


def padded_rows(ref, scratch):
    scratch[...] = jnp.zeros_like(scratch)
    scratch[0 : ref.shape[0], :] = ref[...].astype(F32)
    return scratch[...]


def attention_kernel(
    rows_ref,
    dec_ref,
    cache_hbm,
    length_ref,
    gain_ref,
    qkv_hbm,
    wo_hbm,
    att_ref,
    dec_att_ref,
    wo_ref,
    g,
    wqkv,
    cache,
    heads,
    dec8,
    dec_out,
    dec_in,
    send,
    recv,
    local_sem,
):
    here = Place()
    rows, width = rows_ref.shape
    hw = width // 2
    blk_count = lax.axis_size("blk")
    score_scale = 1.0 / math.sqrt(HEAD_DIM)
    w_copy = pltpu.make_async_copy(qkv_hbm, wqkv.at[0], local_sem.at[0])
    o_copy = pltpu.make_async_copy(wo_hbm, wo_ref.at[pl.ds(0, HEAD_DIM)], local_sem.at[2])
    c_copy = pltpu.make_async_copy(cache_hbm, cache, local_sem.at[1])
    w_copy.start()
    o_copy.start()
    c_copy.start()
    core, y = here.b % 2, here.b // 2
    blk_peers = []
    if blk_count > 1:
        blk_peers = [(here.b + 1 - 2 * core, here.e)]
        blk_peers += [(((y + k) % 4) * 2 + core, here.e) for k in (1, 3, 2)]
    wait_all = greet([here.mate(), here.other(), here.at(0, 1), here.at(0, 3)] + blk_peers)
    own = normed(rows_ref[...].astype(F32), gain_ref[...])
    g[0, 0:rows] = own[:, :hw]
    g[1, 0:rows] = own[:, hw:]
    wait_all()
    gather = PairGather(here, g, rows, send, recv)
    gather.open()
    w_half = pl.ds(pl.multiple_of(core * hw, hw), hw)
    o_at = HEAD_DIM + core * (HEAD_DIM // 2)
    o_half = pl.ds(pl.multiple_of(o_at, HEAD_DIM // 2), HEAD_DIM // 2)
    o_src = pl.ds(pl.multiple_of(core * (HEAD_DIM // 2), HEAD_DIM // 2), HEAD_DIM // 2)
    fetch, share = [], []
    if blk_count > 1:
        for i, (src, dst) in enumerate(
            ((qkv_hbm.at[:, w_half], wqkv.at[1, :, w_half]), (wo_hbm.at[o_src], wo_ref.at[o_half]))
        ):
            fetch.append(remote(src, dst, send, recv, 36 + i, here.other()))
            share.append(remote(dst, dst, send, recv, 38 + i, blk_peers[0]))
    else:
        for i, (src, dst) in enumerate(
            ((qkv_hbm, wqkv.at[1]), (wo_hbm, wo_ref.at[pl.ds(HEAD_DIM, HEAD_DIM)]))
        ):
            fetch.append(remote(src, dst, send, recv, 36 + i, here.other()))
    for copy in fetch:
        copy.start()

    dn = normed(padded_rows(dec_ref, dec8), gain_ref[...])
    w_copy.wait()
    q8 = nn(dn, wqkv[0, 0]).astype(BF16)
    k8 = nn(dn, wqkv[0, 1]).astype(BF16)
    v8 = nn(dn, wqkv[0, 2]).astype(BF16)
    c_copy.wait()
    count = cache.shape[1]
    span = cache.shape[2]
    row = lax.broadcasted_iota(jnp.int32, (8, 1), 0)
    scores = jnp.zeros((8, span), F32)
    lengths = jnp.zeros((8, 1), jnp.int32)
    for d in range(count):
        scores = jnp.where(row == d, nt(q8, cache[0, d]), scores)
        lengths = jnp.where(row == d, length_ref[d], lengths)
    position = here.b * span + lax.broadcasted_iota(jnp.int32, (8, span), 1)
    valid = position < lengths
    masked = jnp.where(valid, scores * score_scale, -1e30)
    top = jnp.max(masked, axis=-1, keepdims=True)
    weights = jnp.where(valid, jnp.exp(masked - top), 0.0)
    total = jnp.sum(weights, axis=-1, keepdims=True)
    coarse = weights.astype(BF16).astype(F32)
    both = jnp.concatenate([coarse, weights - coarse], axis=0).astype(BF16)
    mix = jnp.zeros((8, HEAD_DIM), F32)
    for d in range(count):
        pair = nn(both, cache[1, d])
        mix = jnp.where(row == d, pair[0:8] + pair[8:16], mix)

    def pack(at, mix, top, total):
        dec_out[at, 0:8] = mix
        dec_out[at, 8:16] = jnp.broadcast_to(top, (8, HEAD_DIM))
        dec_out[at, 16:24] = jnp.broadcast_to(total, (8, HEAD_DIM))

    def merge(mix, top, total, at):
        other_top = dec_in[at, 8:16]
        new_top = jnp.maximum(top, other_top)
        mine, theirs = jnp.exp(top - new_top), jnp.exp(other_top - new_top)
        return (
            mix * mine + dec_in[at, 0:8] * theirs,
            new_top,
            total * mine + dec_in[at, 16:24] * theirs,
        )

    top = jnp.broadcast_to(top, (8, HEAD_DIM))
    total = jnp.broadcast_to(total, (8, HEAD_DIM))
    pack(0, mix, top, total)
    blk_copies = [
        remote(dec_out.at[min(k, 1)], dec_in.at[k], send, recv, 40 + k, peer)
        for k, peer in enumerate(blk_peers)
    ]
    for copy in blk_copies[:1]:
        copy.start()

    def project(batch, head):
        n = len(PAIR_BATCHES[batch])
        lo, size = batch * n * rows, n * rows
        left, right = g[0, lo : lo + size], g[1, lo : lo + size]
        for which in range(3):
            w = wqkv.at[head, which]
            out = (nn(left, w[0:hw]) + nn(right, w[hw:width])).astype(BF16)
            for j, place in enumerate(PAIR_BATCHES[batch]):
                at = pl.multiple_of(here.block(place) * rows, rows)
                heads[head, which, pl.ds(at, rows)] = out[j * rows : (j + 1) * rows]

    gather.to_batch_0()
    project(0, 0)
    gather.relay()
    for copy in fetch:
        copy.wait_recv()
    for copy in share:
        copy.start()
    if blk_copies:
        blk_copies[0].wait_recv()
        mix, top, total = merge(mix, top, total, 0)
        pack(1, mix, top, total)
        for copy in blk_copies[1:]:
            copy.start()
    for copy in share:
        copy.wait_recv()
    project(0, 1)
    gather.to_batch_1()
    project(1, 0)
    project(1, 1)
    for k, copy in enumerate(blk_copies[1:]):
        copy.wait_recv()
        mix, top, total = merge(mix, top, total, k + 1)
    q32, k32, v32 = q8.astype(F32), k8.astype(F32), v8.astype(F32)
    new_score = jnp.sum(q32 * k32, axis=-1, keepdims=True) * score_scale
    new_top = jnp.maximum(top, new_score)
    old = jnp.exp(top - new_top)
    fresh = jnp.exp(new_score - new_top)
    dec_att_ref[...] = ((mix * old + fresh * v32) / (total * old + fresh)).astype(BF16)

    step = 256
    diagonal = lax.broadcasted_iota(jnp.int32, (step, step), 0) >= lax.broadcasted_iota(
        jnp.int32, (step, step), 1
    )

    def one_head(head, carry):
        lanes = pl.ds(pl.multiple_of(head * HEAD_DIM, HEAD_DIM), HEAD_DIM)
        for qb in range(REQUEST_LEN // step):
            at = qb * step
            q = heads[head, 0, at : at + step]
            s1 = jnp.where(diagonal, nt(q, heads[head, 1, at : at + step]) * score_scale, -jnp.inf)
            top_q = jnp.max(s1, axis=-1, keepdims=True)
            if qb:
                s0 = nt(q, heads[head, 1, 0:at]) * score_scale
                top_q = jnp.maximum(top_q, jnp.max(s0, axis=-1, keepdims=True))
            p1 = jnp.exp(s1 - top_q)
            sum_q = jnp.sum(p1, axis=-1, keepdims=True)
            out = nn(p1.astype(BF16), heads[head, 2, at : at + step])
            if qb:
                p0 = jnp.exp(s0 - top_q)
                sum_q = sum_q + jnp.sum(p0, axis=-1, keepdims=True)
                out = out + nn(p0.astype(BF16), heads[head, 2, 0:at])
            att_ref[at : at + step, lanes] = (out / sum_q).astype(BF16)
        return carry

    lax.fori_loop(0, 2, one_head, 0)
    o_copy.wait()
    for copy in fetch + share:
        copy.wait_send()
    gather.close()
    for copy in blk_copies:
        copy.wait_send()


def layer_kernel(
    rows_ref,
    dec_ref,
    att_ref,
    dec_att_ref,
    gain_ref,
    wo_ref,
    routes_ref,
    weight_ref,
    dec_routes_ref,
    dec_weight_ref,
    gate_ref,
    wgu_hbm,
    wd_hbm,
    wst_hbm,
    wsd_hbm,
    out_ref,
    dec_out_ref,
    g,
    part,
    fwd,
    full,
    wgu,
    wd,
    wsp,
    wsd,
    xe,
    he,
    ye,
    hs,
    gv,
    wslot,
    pick,
    back,
    meta,
    dec8,
    dec_send,
    dec_recv,
    res,
    send,
    recv,
    local_sem,
):
    here = Place()
    rows, width = rows_ref.shape
    hw = width // 2
    cap = pick.shape[1]
    ff = wd.shape[0]
    sff = wsd_hbm.shape[0]
    count = dec_ref.shape[0]
    tail = sff - 256
    tile = min(256, hw)

    moves = [(wgu_hbm, wgu), (wd_hbm, wd), (wsd_hbm, wsd.at[pl.ds(0, sff)])]
    for group, size in enumerate((128, 128, tail)):
        for kind in range(2):
            moves.append(
                (
                    wst_hbm.at[kind, pl.ds(group * 128, size)],
                    wsp.at[pl.ds(group * 256 + kind * 128, size)],
                )
            )
    local = [pltpu.make_async_copy(a, b, local_sem.at[i]) for i, (a, b) in enumerate(moves)]
    for copy in local:
        copy.start()
    peers = [here.at(1, 0), here.at(3, 0), here.at(0, 1), here.at(0, 3), here.at(2, 0), here.at(0, 2)]
    wait_all = greet(peers)

    weight = weight_ref[...]
    coarse = weight.astype(BF16).astype(F32)
    meta[0, 0] = jnp.concatenate(
        [routes_ref[...].astype(F32), coarse, weight - coarse, jnp.zeros_like(weight)], axis=0
    ).astype(BF16)

    def out_project(*places):
        for place in places:
            at = pl.multiple_of(here.block(place) * rows, rows)
            term = nn(att_ref[pl.ds(at, rows)], wo_ref[...]).astype(BF16)
            part[0, PAIR[place]] = term[:, :hw]
            part[1, PAIR[place]] = term[:, hw:]

    first = PairScatter(here, part, fwd, full, send, recv)
    gather = Gather(here, g, rows, send, recv, 40)
    second = Scatter(here, part, fwd, full, send, recv, 80)

    def exchange(buf_send, buf_recv, base, along):
        steps = ((1, 0), (3, 0), (2, 0)) if along == 0 else ((0, 1), (0, 3), (0, 2))
        return [
            remote(buf_send, buf_recv.at[k], send, recv, base + k, here.at(*step))
            for k, step in enumerate(steps)
        ]

    meta_z = [
        remote(meta.at[0, 0], meta.at[0, dst], send, recv, 120 + k, here.at(0, dz))
        for k, (dz, dst) in enumerate(((1, 3), (3, 1), (2, 2)))
    ]
    meta_x = [
        remote(meta.at[0], meta.at[dst], send, recv, 123 + k, here.at(dx, 0))
        for k, (dx, dst) in enumerate(((1, 3), (3, 1), (2, 2)))
    ]
    dec_copies = [
        exchange(dec_send.at[k], dec_recv.at[k], 126 + 3 * k, 1 - k % 2) for k in range(4)
    ]

    out_project((1, 2))
    dec_term = nn(dec_att_ref[...], wo_ref[0:HEAD_DIM])
    dec_send[0] = dec_term.astype(BF16)
    wait_all()
    first.start(("m", 0, 2))
    first.far(1, 1)
    for copy in meta_z + dec_copies[0]:
        copy.start()
    out_project((1, 1))
    first.start(("m", 0, 1))
    out_project((0, 2))
    first.far(1, 0)
    out_project((1, 3))
    first.start(("m", 0, 3))
    first.pass_plus(1, 1)
    first.pass_minus(1, 1)
    out_project((1, 0))
    first.start(("m", 0, 0))
    out_project((0, 1), (0, 3))
    first.pass_plus(1, 0)
    first.pass_minus(1, 0)
    out_project((0, 0))

    def dec_sum(k):
        total = dec_send[k].astype(F32)
        for copy in dec_copies[k]:
            copy.wait_recv()
        for at in range(3):
            total = total + dec_recv[k, at].astype(F32)
        return total

    for copy in meta_z:
        copy.wait_recv()
    for copy in meta_x:
        copy.start()
    dec_send[1] = dec_sum(0).astype(BF16)
    for copy in dec_copies[1]:
        copy.start()

    gate = gate_ref[...]
    gate_coarse = gate.astype(BF16).astype(F32)
    for copy in local:
        copy.wait()
    pad = 128 - tail
    row_at = lax.broadcasted_iota(jnp.int32, (pad, width), 0)
    wsp[512 + tail : 640] = jnp.where(
        row_at == 0, gate_coarse, jnp.where(row_at == 1, gate - gate_coarse, 0.0)
    ).astype(BF16)
    wsp[640 + tail : 768] = jnp.zeros((pad, width), BF16)
    wsd[sff : wsd.shape[0]] = jnp.zeros((wsd.shape[0] - sff, width), BF16)

    for copy in meta_x:
        copy.wait_recv()
    expert = here.e.astype(F32)
    iota_r = lax.broadcasted_iota(jnp.int32, (rows, rows), 0)
    iota_c = lax.broadcasted_iota(jnp.int32, (rows, rows), 1)
    upper = (iota_r <= iota_c).astype(F32).astype(BF16)
    eye = (iota_r == iota_c).astype(F32).astype(BF16)
    iota_cap = lax.broadcasted_iota(jnp.int32, (cap, rows), 0).astype(F32)
    iota_lane = iota_c.astype(F32)
    for place, at in SLOT.items():
        info = meta[place[0], place[1]].astype(F32)
        match = info[0:4] == expert
        chosen = jnp.sum(match.astype(F32), axis=0, keepdims=True)
        scale = jnp.sum(jnp.where(match, info[4:8] + info[8:12], 0.0), axis=0, keepdims=True)
        order = nn(jnp.broadcast_to(chosen, (8, rows)).astype(BF16), upper)[0:1] - 1.0
        order = jnp.where(chosen > 0.0, order, -1.0)
        choice = iota_cap == order
        pick[at] = choice.astype(F32).astype(BF16)
        wslot[at] = jnp.broadcast_to(
            jnp.sum(jnp.where(choice, scale, 0.0), axis=1, keepdims=True), (cap, 128)
        )
        column = nt(eye, jnp.broadcast_to(order, (8, rows)).astype(BF16))[:, 0:1]
        back[at] = (iota_lane == column).astype(F32).astype(BF16)

    dec_res = (padded_rows(dec_ref, dec8) + dec_sum(1)).astype(BF16).astype(F32)
    dec_two = normed(dec_res, gain_ref[...])
    dec8[...] = dec_res
    base_row = 16 * rows
    dec_pad = jnp.concatenate([dec_two.astype(F32), jnp.zeros((8, width), F32)], axis=0).astype(BF16)
    g[0, base_row : base_row + 16] = dec_pad[:, :hw]
    g[1, base_row : base_row + 16] = dec_pad[:, hw:]

    halves = first.finish()
    sum_sq = jnp.zeros((rows, 1), F32)
    for half in range(2):
        cols = pl.ds(half * hw, hw)
        value = (rows_ref[:, cols].astype(F32) + halves[half]).astype(BF16)
        res[:, cols] = value
        wide = value.astype(F32)
        sum_sq = sum_sq + jnp.sum(wide * wide, axis=-1, keepdims=True)
    factor = lax.rsqrt(sum_sq / width + EPS)
    for half in range(2):
        cols = pl.ds(half * hw, hw)
        g[half, 0:rows] = (res[:, cols].astype(F32) * factor * gain_ref[:, cols]).astype(BF16)
    gather.open()
    first.close()

    row8 = lax.broadcasted_iota(jnp.int32, (16, 1), 0)
    dec_scale = jnp.zeros((16, 1), F32)
    for d in range(count):
        one = jnp.float32(0.0)
        for k in range(dec_routes_ref.shape[1]):
            one = one + jnp.where(dec_routes_ref[d, k] == here.e, dec_weight_ref[d, k], 0.0)
        dec_scale = jnp.where(row8 == d, one, dec_scale)

    def feed_forward(batch):
        places = BATCHES[batch]
        start, n = STARTS[batch], len(places)
        decode = batch == 2
        extra = 16 if decode else 0
        m, me = n * rows + extra, n * cap + extra
        lo = start * rows
        for j in range(n):
            at = lo + j * rows
            for half in range(2):
                xe[j * cap : (j + 1) * cap, half * hw : (half + 1) * hw] = nn(
                    pick[start + j], g[half, at : at + rows]
                ).astype(BF16)
        if decode:
            xe[n * cap : me] = dec_pad

        def up(i, carry):
            at = pl.multiple_of(i * 128, 128)
            w = jnp.concatenate([wgu[:, pl.ds(at, 128)], wgu[:, pl.ds(ff + at, 128)]], axis=1)
            hidden = nn(xe[0:me], w)
            he[0:me, pl.ds(at, 128)] = (silu(hidden[:, 0:128]) * hidden[:, 128:256]).astype(BF16)
            return carry

        lax.fori_loop(0, ff // 128, up, 0)

        scale = jnp.concatenate(
            [wslot[start + j][:, 0:1] for j in range(n)] + ([dec_scale] if decode else []), axis=0
        )

        def down(i, carry):
            cols = pl.ds(pl.multiple_of(i * tile, tile), tile)
            ye[0:me, cols] = (nn(he[0:me], wd[:, cols]) * scale).astype(BF16)
            return carry

        lax.fori_loop(0, width // tile, down, 0)

        for group in range(3):
            w = wsp.at[pl.ds(group * 256, 256)]
            hidden = nt(g[0, lo : lo + m], w[:, 0:hw]) + nt(g[1, lo : lo + m], w[:, hw:width])
            hs[0:m, group * 128 : (group + 1) * 128] = (
                silu(hidden[:, 0:128]) * hidden[:, 128:256]
            ).astype(BF16)
            if group == 2:
                logit = hidden[:, tail : tail + 1] + hidden[:, tail + 1 : tail + 2]
                gv[0:m] = jnp.broadcast_to(1.0 / (1.0 + jnp.exp(-logit)), (m, 128))

        for half in range(2):

            def combine(i, carry, half=half):
                here_cols = pl.ds(pl.multiple_of(i * tile, tile), tile)
                cols = pl.ds(pl.multiple_of(half * hw + i * tile, tile), tile)
                shared = nn(hs[0:m], wsd[:, cols]) * gv[0:m, 0:1]
                for j in range(n):
                    routed = nn(back[start + j][:, 0:cap], ye[j * cap : (j + 1) * cap, cols])
                    part[half, start + j, :, here_cols] = (
                        shared[j * rows : (j + 1) * rows] + routed
                    ).astype(BF16)
                if decode:
                    dec_send[2, :, cols] = (
                        shared[n * rows : n * rows + 8] + ye[n * cap : n * cap + 16, cols].astype(F32)[0:8]
                    ).astype(BF16)
                return carry

            lax.fori_loop(0, hw // tile, combine, 0)

    gather.to_batch_0()
    feed_forward(0)
    gather.to_batch_1()
    feed_forward(1)
    second.send_far(0)
    gather.to_batch_2()
    second.pass_on(0)
    feed_forward(2)
    second.send_far(2, 1, 3)
    for copy in dec_copies[2]:
        copy.start()
    second.pass_on(2, 1, 3)
    dec_send[3] = dec_sum(2).astype(BF16)
    for copy in dec_copies[3]:
        copy.start()
    halves = second.finish()
    for half in range(2):
        cols = pl.ds(half * hw, hw)
        out_ref[:, cols] = (res[:, cols].astype(F32) + halves[half]).astype(BF16)
    dec_out_ref[...] = (dec8[...] + dec_sum(3)).astype(BF16)[0:count]
    gather.close()
    second.close()
    for copy in meta_z + meta_x + sum(dec_copies, []):
        copy.wait_send()


def per_device(
    prefill_rows,
    decode_rows,
    key_values,
    cache_length,
    attention_gain,
    feedforward_gain,
    query_key_value,
    out_projection,
    routes,
    route_weight,
    decode_routes,
    decode_weight,
    expert_gate_up,
    expert_down,
    shared_gate_up,
    shared_down,
    shared_gate,
):
    rows, width = prefill_rows.shape
    hw = width // 2
    tokens = rows * 16
    count, span = decode_rows.shape[0], key_values.shape[2]
    cap = 3 * rows * routes.shape[1] // 32
    ff = expert_down.shape[1]
    vmem = pl.BlockSpec(memory_space=pltpu.VMEM)
    smem = pl.BlockSpec(memory_space=pltpu.SMEM)
    hbm = pl.BlockSpec(memory_space=pl.ANY)
    most = max(len(b) for b in BATCHES)
    attended, decode_attended, projection = pl.pallas_call(
        attention_kernel,
        out_shape=(
            jax.ShapeDtypeStruct((tokens // 2, 2 * HEAD_DIM), BF16),
            jax.ShapeDtypeStruct((8, HEAD_DIM), BF16),
            jax.ShapeDtypeStruct((2 * HEAD_DIM, width), BF16),
        ),
        in_specs=[vmem, vmem, hbm, smem, vmem, hbm, hbm],
        out_specs=(vmem, vmem, vmem),
        scratch_shapes=[
            pltpu.VMEM((2, tokens // 2, hw), BF16),
            pltpu.VMEM((2, 3, width, HEAD_DIM), BF16),
            pltpu.VMEM((2, count, span, HEAD_DIM), BF16),
            pltpu.VMEM((2, 3, tokens // 2, HEAD_DIM), BF16),
            pltpu.VMEM((8, width), F32),
            pltpu.VMEM((2, 24, HEAD_DIM), F32),
            pltpu.VMEM((4, 24, HEAD_DIM), F32),
            pltpu.SemaphoreType.DMA((44,)),
            pltpu.SemaphoreType.DMA((44,)),
            pltpu.SemaphoreType.DMA((3,)),
        ],
        compiler_params=pltpu.CompilerParams(
            collective_id=0, has_side_effects=True, vmem_limit_bytes=67043328
        ),
        name="attend",
    )(
        prefill_rows,
        decode_rows,
        key_values,
        cache_length,
        attention_gain.reshape(1, width),
        jnp.transpose(query_key_value, (1, 0, 2)),
        out_projection,
    )
    return pl.pallas_call(
        layer_kernel,
        out_shape=(
            jax.ShapeDtypeStruct((rows, width), BF16),
            jax.ShapeDtypeStruct((count, width), BF16),
        ),
        in_specs=[vmem] * 8 + [smem] * 2 + [vmem] + [hbm] * 4,
        out_specs=(vmem, vmem),
        scratch_shapes=[
            pltpu.VMEM((2, tokens + 16, hw), BF16),
            pltpu.VMEM((2, 16, rows, hw), BF16),
            pltpu.VMEM((2, 5, 2, rows // 2, hw), BF16),
            pltpu.VMEM((2, 5, 2, rows, hw), BF16),
            pltpu.VMEM((width, 2 * ff), BF16),
            pltpu.VMEM((ff, width), BF16),
            pltpu.VMEM((768, width), BF16),
            pltpu.VMEM((384, width), BF16),
            pltpu.VMEM((most * cap + 16, width), BF16),
            pltpu.VMEM((most * cap + 16, ff), BF16),
            pltpu.VMEM((most * cap + 16, width), BF16),
            pltpu.VMEM((most * rows + 16, 384), BF16),
            pltpu.VMEM((most * rows + 16, 128), F32),
            pltpu.VMEM((16, cap, 128), F32),
            pltpu.VMEM((16, cap, rows), BF16),
            pltpu.VMEM((16, rows, rows), BF16),
            pltpu.VMEM((4, 4, 16, rows), BF16),
            pltpu.VMEM((8, width), F32),
            pltpu.VMEM((4, 8, width), BF16),
            pltpu.VMEM((4, 3, 8, width), BF16),
            pltpu.VMEM((rows, width), BF16),
            pltpu.SemaphoreType.DMA((138,)),
            pltpu.SemaphoreType.DMA((138,)),
            pltpu.SemaphoreType.DMA((9,)),
        ],
        compiler_params=pltpu.CompilerParams(
            collective_id=1, has_side_effects=True, vmem_limit_bytes=67043328
        ),
        name="layer",
    )(
        prefill_rows,
        decode_rows,
        attended,
        decode_attended,
        feedforward_gain.reshape(1, width),
        projection,
        routes.T,
        route_weight.T,
        decode_routes,
        decode_weight,
        shared_gate.reshape(1, width),
        expert_gate_up[0],
        expert_down[0],
        jnp.transpose(shared_gate_up, (1, 2, 0)),
        shared_down,
    )


def solution(mesh):
    return jax.shard_map(
        per_device,
        mesh=mesh,
        in_specs=(
            P(("blk", "expert"), None),
            P(),
            P(None, None, "blk", "expert"),
            P(),
            P(),
            P(),
            P(None, None, "expert"),
            P("expert", None),
            P(("blk", "expert"), None),
            P(("blk", "expert"), None),
            P(),
            P(),
            P("expert", None, None),
            P("expert", None, None),
            P(None, None, "expert"),
            P("expert", None),
            P(),
        ),
        out_specs=(P(("blk", "expert"), None), P()),
        check_vma=False,
    )
```

```python
import math

import jax
import jax.numpy as jnp
from jax import lax
from jax.experimental import pallas as pl
from jax.experimental.pallas import tpu as pltpu
from jax.sharding import PartitionSpec as P

HEAD_DIM = 128
REQUEST_LEN = 1024
EPS = 1e-06
MESH = pl.DeviceIdType.MESH
F32 = jnp.float32
BF16 = jnp.bfloat16

BATCHES = (
    ((0, 0), (0, 1), (0, 3), (1, 0), (3, 0)),
    ((1, 1), (1, 3), (3, 1), (3, 3), (2, 0), (0, 2)),
    ((1, 2), (2, 1)),
    ((3, 2), (2, 3), (2, 2)),
)
SLOT = {place: at for at, place in enumerate(sum(BATCHES, ()))}
STARTS = (0, 5, 11, 13)
PAIR_BATCHES = (((0, 0), (0, 1), (0, 3), (1, 0)), ((0, 2), (1, 1), (1, 3), (1, 2)))
PAIR = {place: at for at, place in enumerate(sum(PAIR_BATCHES, ()))}


def nn(a, b):
    return lax.dot_general(a, b, (((1,), (0,)), ((), ())), preferred_element_type=F32)


def nt(a, b):
    return lax.dot_general(a, b, (((1,), (1,)), ((), ())), preferred_element_type=F32)


def normed(values, gain):
    factor = lax.rsqrt(jnp.mean(values * values, axis=-1, keepdims=True) + EPS)
    return (values * factor * gain).astype(BF16)


def silu(v):
    return v * (1.0 / (1.0 + jnp.exp(-v)))


class Place:
    def __init__(self):
        self.b = lax.axis_index("blk")
        self.e = lax.axis_index("expert")
        self.x = self.e // 4
        self.z = self.e % 4

        odd = self.x % 2
        self.mate = lambda: self.at(1 + 2 * odd, 0)
        self.other = lambda: self.at(3 - 2 * odd, 0)
        self.odd = odd

    def at(self, dx, dz):
        return (self.b, ((self.x + dx) % 4) * 4 + (self.z + dz) % 4)

    def block(self, place):
        half = self.odd if place[0] == 0 else 1 - self.odd
        return half * 4 + (self.z + place[1]) % 4


def greet(peers):
    barrier = pltpu.get_barrier_semaphore()
    for peer in peers:
        pl.semaphore_signal(barrier, inc=1, device_id=peer, device_id_type=MESH)
    return lambda: pl.semaphore_wait(barrier, len(peers))


def remote(src, dst, send, recv, at, device):
    return pltpu.make_async_remote_copy(
        src_ref=src,
        dst_ref=dst,
        send_sem=send.at[at],
        recv_sem=recv.at[at],
        device_id=device,
        device_id_type=MESH,
    )


def slot(half, p, q):
    return SLOT[(p, q) if half == 0 else (q, p)]


def sides(here, half):
    along_x = (here.at(1, 0), here.at(3, 0))
    along_z = (here.at(0, 1), here.at(0, 3))
    return along_x + along_z if half == 0 else along_z + along_x


class Gather:
    def __init__(self, here, rows_ref, rows, send, recv, base):
        self.copies = []
        hr = rows // 2
        for half in range(2):
            major_p, major_m, minor_p, minor_m = sides(here, half)
            c = {}

            def put(name, at, src, dst, part, device):
                lo, size = part
                c[name] = remote(
                    rows_ref.at[half, pl.ds(slot(half, *src) * rows + lo, size)],
                    rows_ref.at[half, pl.ds(slot(half, *dst) * rows + lo, size)],
                    send,
                    recv,
                    base + half * 20 + at,
                    device,
                )

            whole, low, high = (0, rows), (0, hr), (hr, hr)
            put("n+", 0, (0, 0), (0, 3), whole, minor_p)
            put("n-", 1, (0, 0), (0, 1), whole, minor_m)
            put("fn+", 4, (0, 3), (0, 2), high, minor_p)
            put("fn-", 5, (0, 1), (0, 2), low, minor_m)
            for q, at in ((0, 2), (1, 6), (3, 8), (2, 10)):
                put(("j+", q), at, (0, q), (3, q), whole, major_p)
                put(("j-", q), at + 1, (0, q), (1, q), whole, major_m)
            for q, at in ((0, 12), (1, 14), (3, 16), (2, 18)):
                put(("f+", q), at, (3, q), (2, q), high, major_p)
                put(("f-", q), at + 1, (1, q), (2, q), low, major_m)
            self.copies.append(c)

    def start(self, *names):
        for c in self.copies:
            for name in names:
                c[name].start()

    def got(self, *names):
        for c in self.copies:
            for name in names:
                c[name].wait_recv()

    def open(self):
        self.start("n+", "n-", ("j+", 0), ("j-", 0))

    def to_batch_0(self):
        self.got("n+", "n-")
        self.start("fn+", "fn-", ("j+", 1), ("j-", 1), ("j+", 3), ("j-", 3))
        self.got(("j+", 0), ("j-", 0))
        self.start(("f+", 0), ("f-", 0))

    def to_batch_1(self):
        self.got("fn+", "fn-")
        self.start(("j+", 2), ("j-", 2))
        self.got(("j+", 1), ("j-", 1))
        self.start(("f+", 1), ("f-", 1))
        self.got(("j+", 3), ("j-", 3))
        self.start(("f+", 3), ("f-", 3))
        self.got(("f+", 0), ("f-", 0))

    def to_batch_2(self):
        self.got(("j+", 2), ("j-", 2))
        self.start(("f+", 2), ("f-", 2))
        self.got(("f+", 1), ("f-", 1))

    def to_batch_3(self):
        for q in (3, 2):
            self.got(("f+", q), ("f-", q))

    def close(self):
        for c in self.copies:
            for copy in c.values():
                copy.wait_send()


class PairGather:
    def __init__(self, here, rows_ref, rows, send, recv):
        hr = rows // 2
        self.c = c = {}
        z_p, z_m, mate = here.at(0, 1), here.at(0, 3), here.mate()

        def put(name, half, src, dst, lo, size, device):
            c[name] = remote(
                rows_ref.at[half, pl.ds(PAIR[src] * rows + lo, size)],
                rows_ref.at[half, pl.ds(PAIR[dst] * rows + lo, size)],
                send,
                recv,
                len(c),
                device,
            )

        for half, a in ((0, 0), (1, 0), (1, 1)):
            put(("+", half, a), half, (a, 0), (a, 3), 0, rows, z_p)
            put(("-", half, a), half, (a, 0), (a, 1), 0, rows, z_m)
            put(("f+", half, a), half, (a, 3), (a, 2), hr, hr, z_p)
            put(("f-", half, a), half, (a, 1), (a, 2), 0, hr, z_m)
        for q in (0, 1, 3, 2):
            put(("m", 0, q), 0, (0, q), (1, q), 0, rows, mate)
        put(("m", 1, 0), 1, (0, 0), (1, 0), 0, rows, mate)

    def start(self, *names):
        for name in names:
            self.c[name].start()

    def got(self, *names):
        for name in names:
            self.c[name].wait_recv()

    def open(self):
        self.start(("+", 0, 0), ("-", 0, 0), ("m", 1, 0), ("m", 0, 0), ("+", 1, 0), ("-", 1, 0))

    def to_batch_0(self):
        self.got(("+", 0, 0), ("-", 0, 0))
        self.start(("f+", 0, 0), ("f-", 0, 0), ("m", 0, 1), ("m", 0, 3))
        self.got(("m", 1, 0))
        self.start(("+", 1, 1), ("-", 1, 1))
        self.got(("+", 1, 0), ("-", 1, 0))
        self.start(("f+", 1, 0), ("f-", 1, 0))
        self.got(("m", 0, 0))

    def relay(self):
        self.got(("f+", 0, 0), ("f-", 0, 0))
        self.start(("m", 0, 2))
        self.got(("+", 1, 1), ("-", 1, 1))
        self.start(("f+", 1, 1), ("f-", 1, 1))

    def to_batch_1(self):
        self.got(("m", 0, 1), ("m", 0, 3), ("m", 0, 2))
        self.got(("f+", 1, 0), ("f-", 1, 0), ("f+", 1, 1), ("f-", 1, 1))

    def close(self):
        for copy in self.c.values():
            copy.wait_send()


class PairScatter:
    def __init__(self, here, part_ref, fwd_ref, full_ref, send, recv):
        self.part, self.fwd, self.full = part_ref, fwd_ref, full_ref
        self.c = c = {}
        rows = part_ref.shape[2]
        hr = rows // 2
        self.low, self.high = pl.ds(0, hr), pl.ds(hr, hr)
        z_p, z_m, mate = here.at(0, 1), here.at(0, 3), here.mate()

        def put(name, src, dst, device):
            c[name] = remote(src, dst, send, recv, len(c), device)

        for half, a, k in ((0, 0, 4), (1, 1, 1), (1, 0, 0)):
            far, plus, minus = PAIR[a, 2], PAIR[a, 1], PAIR[a, 3]
            put(("f+", half, a), part_ref.at[half, far, self.low], fwd_ref.at[half, k, 0], z_p)
            put(("f-", half, a), part_ref.at[half, far, self.high], fwd_ref.at[half, k, 1], z_m)
            put(("t+", half, a), part_ref.at[half, plus], full_ref.at[half, k, 0], z_p)
            put(("t-", half, a), part_ref.at[half, minus], full_ref.at[half, k, 1], z_m)
        for q in range(4):
            put(("m", 0, q), part_ref.at[0, PAIR[1, q]], full_ref.at[0, q, 0], mate)
        put(("m", 1, 0), part_ref.at[1, PAIR[1, 0]], full_ref.at[1, 4, 0], mate)
        self.slots = {(0, 0): 4, (1, 1): 1, (1, 0): 0}

    def start(self, *names):
        for name in names:
            self.c[name].start()

    def far(self, half, a):
        self.start(("f+", half, a), ("f-", half, a))

    def pass_plus(self, half, a):
        self.c["f+", half, a].wait_recv()
        at, k = PAIR[a, 1], self.slots[half, a]
        self.part[half, at, self.low] = (
            self.part[half, at, self.low].astype(F32) + self.fwd[half, k, 0].astype(F32)
        ).astype(BF16)
        self.c["t+", half, a].start()

    def pass_minus(self, half, a):
        self.c["f-", half, a].wait_recv()
        at, k = PAIR[a, 3], self.slots[half, a]
        self.part[half, at, self.high] = (
            self.part[half, at, self.high].astype(F32) + self.fwd[half, k, 1].astype(F32)
        ).astype(BF16)
        self.c["t-", half, a].start()

    def ring(self, half, a):
        self.c["t+", half, a].wait_recv()
        self.c["t-", half, a].wait_recv()
        k = self.slots[half, a]
        return (
            self.part[half, PAIR[a, 0]].astype(F32)
            + self.full[half, k, 0].astype(F32)
            + self.full[half, k, 1].astype(F32)
        )

    def meet(self, q):
        self.c["m", 0, q].wait_recv()
        at = PAIR[0, q]
        self.part[0, at] = (self.part[0, at].astype(F32) + self.full[0, q, 0].astype(F32)).astype(BF16)

    def finish(self):
        self.meet(2)
        self.far(0, 0)
        self.meet(1)
        self.pass_plus(0, 0)
        self.meet(3)
        self.pass_minus(0, 0)
        self.part[1, PAIR[1, 0]] = self.ring(1, 1).astype(BF16)
        self.start(("m", 1, 0))
        self.meet(0)
        right = self.ring(1, 0)
        left = self.ring(0, 0)
        self.c["m", 1, 0].wait_recv()
        return [left, right + self.full[1, 4, 0].astype(F32)]

    def close(self):
        for copy in self.c.values():
            copy.wait_send()


class Scatter:
    def __init__(self, here, part_ref, fwd_ref, full_ref, send, recv, base):
        self.part, self.fwd, self.full = part_ref, fwd_ref, full_ref
        self.copies = []
        rows = part_ref.shape[2]
        hr = rows // 2
        self.low, self.high = pl.ds(0, hr), pl.ds(hr, hr)
        for half in range(2):
            major_p, major_m, minor_p, minor_m = sides(here, half)
            c = {}

            def put(q, far, plus, minus, side_p, side_m):
                at = base + half * 20 + 4 * q
                c["f+", q] = remote(
                    part_ref.at[half, far, self.low], fwd_ref.at[half, q, 0], send, recv, at, side_p
                )
                c["f-", q] = remote(
                    part_ref.at[half, far, self.high], fwd_ref.at[half, q, 1], send, recv, at + 1, side_m
                )
                c["t+", q] = remote(
                    part_ref.at[half, plus], full_ref.at[half, q, 0], send, recv, at + 2, side_p
                )
                c["t-", q] = remote(
                    part_ref.at[half, minus], full_ref.at[half, q, 1], send, recv, at + 3, side_m
                )

            for q in range(4):
                put(q, slot(half, 2, q), slot(half, 1, q), slot(half, 3, q), major_p, major_m)
            put(4, slot(half, 0, 2), slot(half, 0, 1), slot(half, 0, 3), minor_p, minor_m)
            self.copies.append(c)

    def _next(self, half, q, p):
        return slot(half, p, q) if q < 4 else slot(half, 0, p)

    def send_far(self, *qs):
        for q in qs:
            for half in range(2):
                self.copies[half]["f+", q].start()
                self.copies[half]["f-", q].start()

    def pass_plus(self, half, q):
        c = self.copies[half]
        c["f+", q].wait_recv()
        at = self._next(half, q, 1)
        self.part[half, at, self.low] = (
            self.part[half, at, self.low].astype(F32) + self.fwd[half, q, 0].astype(F32)
        ).astype(BF16)
        c["t+", q].start()

    def pass_minus(self, half, q):
        c = self.copies[half]
        c["f-", q].wait_recv()
        at = self._next(half, q, 3)
        self.part[half, at, self.high] = (
            self.part[half, at, self.high].astype(F32) + self.fwd[half, q, 1].astype(F32)
        ).astype(BF16)
        c["t-", q].start()

    def pass_on(self, *qs):
        for q in qs:
            for half in range(2):
                self.pass_plus(half, q)
                self.pass_minus(half, q)

    def total(self, half, q):
        c = self.copies[half]
        c["t+", q].wait_recv()
        c["t-", q].wait_recv()
        at = self._next(half, q, 0)
        return (
            self.part[half, at].astype(F32)
            + self.full[half, q, 0].astype(F32)
            + self.full[half, q, 1].astype(F32)
        )

    def line(self, q):
        for half in range(2):
            self.part[half, slot(half, 0, q)] = self.total(half, q).astype(BF16)

    def finish(self):
        self.line(2)
        self.send_far(4)
        self.line(1)
        for half in range(2):
            self.pass_plus(half, 4)
        self.line(3)
        for half in range(2):
            self.pass_minus(half, 4)
        self.line(0)
        return [self.total(half, 4) for half in range(2)]

    def close(self):
        for c in self.copies:
            for copy in c.values():
                copy.wait_send()


def padded_rows(ref, scratch):
    scratch[...] = jnp.zeros_like(scratch)
    scratch[0 : ref.shape[0], :] = ref[...].astype(F32)
    return scratch[...]


def attention_kernel(
    rows_hbm,
    dec_ref,
    cache_hbm,
    length_ref,
    gain_ref,
    qkv_hbm,
    wo_hbm,
    att_ref,
    dec_att_ref,
    other_wo,
    rows_ref,
    g,
    wqkv,
    cache,
    heads,
    dec8,
    dec_out,
    dec_in,
    send,
    recv,
    local_sem,
):
    here = Place()
    rows, width = rows_ref.shape
    hw = width // 2
    blk_count = lax.axis_size("blk")
    score_scale = 1.0 / math.sqrt(HEAD_DIM)
    w_copy = pltpu.make_async_copy(qkv_hbm, wqkv.at[0], local_sem.at[0])
    r_copy = pltpu.make_async_copy(rows_hbm, rows_ref, local_sem.at[2])
    r_copy.start()
    c_copy = pltpu.make_async_copy(cache_hbm, cache, local_sem.at[1])
    w_copy.start()
    c_copy.start()
    core, y = here.b % 2, here.b // 2
    blk_peers = []
    if blk_count > 1:
        blk_peers = [(here.b + 1 - 2 * core, here.e)]
        blk_peers += [(((y + k) % 4) * 2 + core, here.e) for k in (1, 3, 2)]
    wait_all = greet([here.mate(), here.other(), here.at(0, 1), here.at(0, 3)] + blk_peers)
    r_copy.wait()
    own = normed(rows_ref[...].astype(F32), gain_ref[...])
    g[0, 0:rows] = own[:, :hw]
    g[1, 0:rows] = own[:, hw:]
    wait_all()
    gather = PairGather(here, g, rows, send, recv)
    gather.open()
    w_half = pl.ds(pl.multiple_of(core * hw, hw), hw)
    o_half = pl.ds(pl.multiple_of(core * (HEAD_DIM // 2), HEAD_DIM // 2), HEAD_DIM // 2)
    fetch, share = [], []
    if blk_count > 1:
        for i, (src, dst) in enumerate(
            ((qkv_hbm.at[:, w_half], wqkv.at[1, :, w_half]), (wo_hbm.at[o_half], other_wo.at[o_half]))
        ):
            fetch.append(remote(src, dst, send, recv, 36 + i, here.other()))
            share.append(remote(dst, dst, send, recv, 38 + i, blk_peers[0]))
    else:
        for i, (src, dst) in enumerate(
            ((qkv_hbm, wqkv.at[1]), (wo_hbm, other_wo))
        ):
            fetch.append(remote(src, dst, send, recv, 36 + i, here.other()))
    for copy in fetch:
        copy.start()

    dn = normed(padded_rows(dec_ref, dec8), gain_ref[...])
    w_copy.wait()
    q8 = nn(dn, wqkv[0, 0]).astype(BF16)
    k8 = nn(dn, wqkv[0, 1]).astype(BF16)
    v8 = nn(dn, wqkv[0, 2]).astype(BF16)
    c_copy.wait()
    count = cache.shape[1]
    span = cache.shape[2]
    row = lax.broadcasted_iota(jnp.int32, (8, 1), 0)
    scores = jnp.zeros((8, span), F32)
    lengths = jnp.zeros((8, 1), jnp.int32)
    for d in range(count):
        scores = jnp.where(row == d, nt(q8, cache[0, d]), scores)
        lengths = jnp.where(row == d, length_ref[d], lengths)
    position = here.b * span + lax.broadcasted_iota(jnp.int32, (8, span), 1)
    valid = position < lengths
    masked = jnp.where(valid, scores * score_scale, -1e30)
    top = jnp.max(masked, axis=-1, keepdims=True)
    weights = jnp.where(valid, jnp.exp(masked - top), 0.0)
    total = jnp.sum(weights, axis=-1, keepdims=True)
    coarse = weights.astype(BF16).astype(F32)
    both = jnp.concatenate([coarse, weights - coarse], axis=0).astype(BF16)
    mix = jnp.zeros((8, HEAD_DIM), F32)
    for d in range(count):
        pair = nn(both, cache[1, d])
        mix = jnp.where(row == d, pair[0:8] + pair[8:16], mix)

    def pack(at, mix, top, total):
        dec_out[at, 0:8] = mix
        dec_out[at, 8:16] = jnp.broadcast_to(top, (8, HEAD_DIM))
        dec_out[at, 16:24] = jnp.broadcast_to(total, (8, HEAD_DIM))

    def merge(mix, top, total, at):
        other_top = dec_in[at, 8:16]
        new_top = jnp.maximum(top, other_top)
        mine, theirs = jnp.exp(top - new_top), jnp.exp(other_top - new_top)
        return (
            mix * mine + dec_in[at, 0:8] * theirs,
            new_top,
            total * mine + dec_in[at, 16:24] * theirs,
        )

    top = jnp.broadcast_to(top, (8, HEAD_DIM))
    total = jnp.broadcast_to(total, (8, HEAD_DIM))
    pack(0, mix, top, total)
    blk_copies = [
        remote(dec_out.at[min(k, 1)], dec_in.at[k], send, recv, 40 + k, peer)
        for k, peer in enumerate(blk_peers)
    ]
    for copy in blk_copies[:1]:
        copy.start()

    def project(batch, head):
        n = len(PAIR_BATCHES[batch])
        lo, size = batch * n * rows, n * rows
        left, right = g[0, lo : lo + size], g[1, lo : lo + size]
        for which in range(3):
            w = wqkv.at[head, which]
            out = (nn(left, w[0:hw]) + nn(right, w[hw:width])).astype(BF16)
            for j, place in enumerate(PAIR_BATCHES[batch]):
                at = pl.multiple_of(here.block(place) * rows, rows)
                heads[head, which, pl.ds(at, rows)] = out[j * rows : (j + 1) * rows]

    gather.to_batch_0()
    project(0, 0)
    gather.relay()
    for copy in fetch:
        copy.wait_recv()
    for copy in share:
        copy.start()
    if blk_copies:
        blk_copies[0].wait_recv()
        mix, top, total = merge(mix, top, total, 0)
        pack(1, mix, top, total)
        for copy in blk_copies[1:]:
            copy.start()
    for copy in share:
        copy.wait_recv()
    project(0, 1)
    gather.to_batch_1()
    project(1, 0)
    project(1, 1)
    for k, copy in enumerate(blk_copies[1:]):
        copy.wait_recv()
        mix, top, total = merge(mix, top, total, k + 1)
    q32, k32, v32 = q8.astype(F32), k8.astype(F32), v8.astype(F32)
    new_score = jnp.sum(q32 * k32, axis=-1, keepdims=True) * score_scale
    new_top = jnp.maximum(top, new_score)
    old = jnp.exp(top - new_top)
    fresh = jnp.exp(new_score - new_top)
    dec_att_ref[...] = ((mix * old + fresh * v32) / (total * old + fresh)).astype(BF16)

    step = 256
    diagonal = lax.broadcasted_iota(jnp.int32, (step, step), 0) >= lax.broadcasted_iota(
        jnp.int32, (step, step), 1
    )

    def one_head(head, carry):
        lanes = pl.ds(pl.multiple_of(head * HEAD_DIM, HEAD_DIM), HEAD_DIM)
        for qb in range(REQUEST_LEN // step):
            at = qb * step
            q = heads[head, 0, at : at + step]
            s1 = jnp.where(diagonal, nt(q, heads[head, 1, at : at + step]) * score_scale, -jnp.inf)
            top_q = jnp.max(s1, axis=-1, keepdims=True)
            if qb:
                s0 = nt(q, heads[head, 1, 0:at]) * score_scale
                top_q = jnp.maximum(top_q, jnp.max(s0, axis=-1, keepdims=True))
            p1 = jnp.exp(s1 - top_q)
            sum_q = jnp.sum(p1, axis=-1, keepdims=True)
            out = nn(p1.astype(BF16), heads[head, 2, at : at + step])
            if qb:
                p0 = jnp.exp(s0 - top_q)
                sum_q = sum_q + jnp.sum(p0, axis=-1, keepdims=True)
                out = out + nn(p0.astype(BF16), heads[head, 2, 0:at])
            att_ref[at : at + step, lanes] = (out / sum_q).astype(BF16)
        return carry

    lax.fori_loop(0, 2, one_head, 0)
    for copy in fetch + share:
        copy.wait_send()
    gather.close()
    for copy in blk_copies:
        copy.wait_send()


def layer_kernel(
    rows_hbm,
    dec_ref,
    att_hbm,
    dec_att_ref,
    gain_ref,
    own_wo,
    other_wo,
    routes_ref,
    weight_ref,
    dec_routes_ref,
    dec_weight_ref,
    gate_ref,
    wgu_hbm,
    wd_hbm,
    wst_hbm,
    wsd_hbm,
    out_ref,
    dec_out_ref,
    rows_ref,
    att_ref,
    wo_ref,
    g,
    part,
    fwd,
    full,
    wgu,
    wd,
    wsp,
    wsd,
    xe,
    he,
    ye,
    hs,
    gv,
    wslot,
    pick,
    back,
    meta,
    dec8,
    dec_send,
    dec_recv,
    res,
    send,
    recv,
    local_sem,
):
    here = Place()
    early = [
        pltpu.make_async_copy(a, b, local_sem.at[9 + i])
        for i, (a, b) in enumerate(
            (
                (att_hbm, att_ref),
                (own_wo, wo_ref.at[pl.ds(0, HEAD_DIM)]),
                (other_wo, wo_ref.at[pl.ds(HEAD_DIM, HEAD_DIM)]),
                (rows_hbm, rows_ref),
            )
        )
    ]
    for copy in early:
        copy.start()
    rows, width = rows_ref.shape
    hw = width // 2
    cap = pick.shape[1]
    ff = wd.shape[0]
    sff = wsd_hbm.shape[0]
    count = dec_ref.shape[0]
    tail = sff - 256
    tile = min(256, hw)

    moves = [(wgu_hbm, wgu), (wd_hbm, wd), (wsd_hbm, wsd.at[pl.ds(0, sff)])]
    for group, size in enumerate((128, 128, tail)):
        for kind in range(2):
            moves.append(
                (
                    wst_hbm.at[kind, pl.ds(group * 128, size)],
                    wsp.at[pl.ds(group * 256 + kind * 128, size)],
                )
            )
    local = [pltpu.make_async_copy(a, b, local_sem.at[i]) for i, (a, b) in enumerate(moves)]
    peers = [here.at(1, 0), here.at(3, 0), here.at(0, 1), here.at(0, 3), here.at(2, 0), here.at(0, 2)]
    wait_all = greet(peers)

    weight = weight_ref[...]
    coarse = weight.astype(BF16).astype(F32)
    meta[0, 0] = jnp.concatenate(
        [routes_ref[...].astype(F32), coarse, weight - coarse, jnp.zeros_like(weight)], axis=0
    ).astype(BF16)

    def out_project(*places):
        for place in places:
            at = pl.multiple_of(here.block(place) * rows, rows)
            term = nn(att_ref[pl.ds(at, rows)], wo_ref[...]).astype(BF16)
            part[0, PAIR[place]] = term[:, :hw]
            part[1, PAIR[place]] = term[:, hw:]

    first = PairScatter(here, part, fwd, full, send, recv)
    gather = Gather(here, g, rows, send, recv, 40)
    second = Scatter(here, part, fwd, full, send, recv, 80)

    def exchange(buf_send, buf_recv, base, along):
        steps = ((1, 0), (3, 0), (2, 0)) if along == 0 else ((0, 1), (0, 3), (0, 2))
        return [
            remote(buf_send, buf_recv.at[k], send, recv, base + k, here.at(*step))
            for k, step in enumerate(steps)
        ]

    meta_z = [
        remote(meta.at[0, 0], meta.at[0, dst], send, recv, 120 + k, here.at(0, dz))
        for k, (dz, dst) in enumerate(((1, 3), (3, 1), (2, 2)))
    ]
    meta_x = [
        remote(meta.at[0], meta.at[dst], send, recv, 123 + k, here.at(dx, 0))
        for k, (dx, dst) in enumerate(((1, 3), (3, 1), (2, 2)))
    ]
    dec_copies = [
        exchange(dec_send.at[k], dec_recv.at[k], 126 + 3 * k, 1 - k % 2) for k in range(4)
    ]

    for copy in early:
        copy.wait()
    out_project((1, 2))
    dec_term = nn(dec_att_ref[...], wo_ref[0:HEAD_DIM])
    dec_send[0] = dec_term.astype(BF16)
    wait_all()
    first.start(("m", 0, 2))
    first.far(1, 1)
    for copy in meta_z + dec_copies[0] + local:
        copy.start()
    out_project((1, 1))
    first.start(("m", 0, 1))
    out_project((0, 2))
    first.far(1, 0)
    out_project((1, 3))
    first.start(("m", 0, 3))
    first.pass_plus(1, 1)
    first.pass_minus(1, 1)
    out_project((1, 0))
    first.start(("m", 0, 0))
    out_project((0, 1), (0, 3))
    first.pass_plus(1, 0)
    first.pass_minus(1, 0)
    out_project((0, 0))

    def dec_sum(k):
        total = dec_send[k].astype(F32)
        for copy in dec_copies[k]:
            copy.wait_recv()
        for at in range(3):
            total = total + dec_recv[k, at].astype(F32)
        return total

    for copy in meta_z:
        copy.wait_recv()
    for copy in meta_x:
        copy.start()
    dec_send[1] = dec_sum(0).astype(BF16)
    for copy in dec_copies[1]:
        copy.start()

    gate = gate_ref[...]
    gate_coarse = gate.astype(BF16).astype(F32)
    for copy in local:
        copy.wait()
    pad = 128 - tail
    row_at = lax.broadcasted_iota(jnp.int32, (pad, width), 0)
    wsp[512 + tail : 640] = jnp.where(
        row_at == 0, gate_coarse, jnp.where(row_at == 1, gate - gate_coarse, 0.0)
    ).astype(BF16)
    wsp[640 + tail : 768] = jnp.zeros((pad, width), BF16)
    wsd[sff : wsd.shape[0]] = jnp.zeros((wsd.shape[0] - sff, width), BF16)

    for copy in meta_x:
        copy.wait_recv()
    expert = here.e.astype(F32)
    iota_r = lax.broadcasted_iota(jnp.int32, (rows, rows), 0)
    iota_c = lax.broadcasted_iota(jnp.int32, (rows, rows), 1)
    upper = (iota_r <= iota_c).astype(F32).astype(BF16)
    eye = (iota_r == iota_c).astype(F32).astype(BF16)
    iota_cap = lax.broadcasted_iota(jnp.int32, (cap, rows), 0).astype(F32)
    iota_lane = iota_c.astype(F32)
    for place, at in SLOT.items():
        info = meta[place[0], place[1]].astype(F32)
        match = info[0:4] == expert
        chosen = jnp.sum(match.astype(F32), axis=0, keepdims=True)
        scale = jnp.sum(jnp.where(match, info[4:8] + info[8:12], 0.0), axis=0, keepdims=True)
        order = nn(jnp.broadcast_to(chosen, (8, rows)).astype(BF16), upper)[0:1] - 1.0
        order = jnp.where(chosen > 0.0, order, -1.0)
        choice = iota_cap == order
        pick[at] = choice.astype(F32).astype(BF16)
        wslot[at] = jnp.broadcast_to(
            jnp.sum(jnp.where(choice, scale, 0.0), axis=1, keepdims=True), (cap, 128)
        )
        column = nt(eye, jnp.broadcast_to(order, (8, rows)).astype(BF16))[:, 0:1]
        back[at] = (iota_lane == column).astype(F32).astype(BF16)

    dec_res = (padded_rows(dec_ref, dec8) + dec_sum(1)).astype(BF16).astype(F32)
    dec_two = normed(dec_res, gain_ref[...])
    dec8[...] = dec_res
    base_row = 16 * rows
    dec_pad = jnp.concatenate([dec_two.astype(F32), jnp.zeros((8, width), F32)], axis=0).astype(BF16)
    g[0, base_row : base_row + 16] = dec_pad[:, :hw]
    g[1, base_row : base_row + 16] = dec_pad[:, hw:]

    halves = first.finish()
    sum_sq = jnp.zeros((rows, 1), F32)
    for half in range(2):
        cols = pl.ds(half * hw, hw)
        value = (rows_ref[:, cols].astype(F32) + halves[half]).astype(BF16)
        res[:, cols] = value
        wide = value.astype(F32)
        sum_sq = sum_sq + jnp.sum(wide * wide, axis=-1, keepdims=True)
    factor = lax.rsqrt(sum_sq / width + EPS)
    for half in range(2):
        cols = pl.ds(half * hw, hw)
        g[half, 0:rows] = (res[:, cols].astype(F32) * factor * gain_ref[:, cols]).astype(BF16)
    gather.open()
    first.close()

    row8 = lax.broadcasted_iota(jnp.int32, (16, 1), 0)
    dec_scale = jnp.zeros((16, 1), F32)
    for d in range(count):
        one = jnp.float32(0.0)
        for k in range(dec_routes_ref.shape[1]):
            one = one + jnp.where(dec_routes_ref[d, k] == here.e, dec_weight_ref[d, k], 0.0)
        dec_scale = jnp.where(row8 == d, one, dec_scale)

    def feed_forward(batch):
        places = BATCHES[batch]
        start, n = STARTS[batch], len(places)
        decode = batch == 3
        extra = 16 if decode else 0
        m, me = n * rows + extra, n * cap + extra
        lo = start * rows
        for j in range(n):
            at = lo + j * rows
            for half in range(2):
                xe[j * cap : (j + 1) * cap, half * hw : (half + 1) * hw] = nn(
                    pick[start + j], g[half, at : at + rows]
                ).astype(BF16)
        if decode:
            xe[n * cap : me] = dec_pad

        def up(i, carry):
            at = pl.multiple_of(i * 128, 128)
            w = jnp.concatenate([wgu[:, pl.ds(at, 128)], wgu[:, pl.ds(ff + at, 128)]], axis=1)
            hidden = nn(xe[0:me], w)
            he[0:me, pl.ds(at, 128)] = (silu(hidden[:, 0:128]) * hidden[:, 128:256]).astype(BF16)
            return carry

        lax.fori_loop(0, ff // 128, up, 0)

        scale = jnp.concatenate(
            [wslot[start + j][:, 0:1] for j in range(n)] + ([dec_scale] if decode else []), axis=0
        )

        def down(i, carry):
            cols = pl.ds(pl.multiple_of(i * tile, tile), tile)
            ye[0:me, cols] = (nn(he[0:me], wd[:, cols]) * scale).astype(BF16)
            return carry

        lax.fori_loop(0, width // tile, down, 0)

        for group in range(3):
            w = wsp.at[pl.ds(group * 256, 256)]
            hidden = nt(g[0, lo : lo + m], w[:, 0:hw]) + nt(g[1, lo : lo + m], w[:, hw:width])
            hs[0:m, group * 128 : (group + 1) * 128] = (
                silu(hidden[:, 0:128]) * hidden[:, 128:256]
            ).astype(BF16)
            if group == 2:
                logit = hidden[:, tail : tail + 1] + hidden[:, tail + 1 : tail + 2]
                gv[0:m] = jnp.broadcast_to(1.0 / (1.0 + jnp.exp(-logit)), (m, 128))

        for half in range(2):

            def combine(i, carry, half=half):
                here_cols = pl.ds(pl.multiple_of(i * tile, tile), tile)
                cols = pl.ds(pl.multiple_of(half * hw + i * tile, tile), tile)
                shared = nn(hs[0:m], wsd[:, cols]) * gv[0:m, 0:1]
                for j in range(n):
                    routed = nn(back[start + j][:, 0:cap], ye[j * cap : (j + 1) * cap, cols])
                    part[half, start + j, :, here_cols] = (
                        shared[j * rows : (j + 1) * rows] + routed
                    ).astype(BF16)
                if decode:
                    dec_send[2, :, cols] = (
                        shared[n * rows : n * rows + 8] + ye[n * cap : n * cap + 16, cols].astype(F32)[0:8]
                    ).astype(BF16)
                return carry

            lax.fori_loop(0, hw // tile, combine, 0)

    gather.to_batch_0()
    feed_forward(0)
    gather.to_batch_1()
    feed_forward(1)
    gather.to_batch_2()
    second.send_far(0)
    feed_forward(2)
    second.send_far(1)
    second.pass_on(0)
    gather.to_batch_3()
    second.pass_on(1)
    feed_forward(3)
    second.send_far(2, 3)
    for copy in dec_copies[2]:
        copy.start()
    second.pass_on(2, 3)
    dec_send[3] = dec_sum(2).astype(BF16)
    for copy in dec_copies[3]:
        copy.start()
    halves = second.finish()
    for half in range(2):
        cols = pl.ds(half * hw, hw)
        out_ref[:, cols] = (res[:, cols].astype(F32) + halves[half]).astype(BF16)
    dec_out_ref[...] = (dec8[...] + dec_sum(3)).astype(BF16)[0:count]
    gather.close()
    second.close()
    for copy in meta_z + meta_x + sum(dec_copies, []):
        copy.wait_send()


def write_kernel(a_ref, b_ref, a_out, b_out):
    a_out[...] = a_ref[...]
    b_out[...] = b_ref[...]


def per_device(
    prefill_rows,
    decode_rows,
    key_values,
    cache_length,
    attention_gain,
    feedforward_gain,
    query_key_value,
    out_projection,
    routes,
    route_weight,
    decode_routes,
    decode_weight,
    expert_gate_up,
    expert_down,
    shared_gate_up,
    shared_down,
    shared_gate,
):
    rows, width = prefill_rows.shape
    hw = width // 2
    tokens = rows * 16
    count, span = decode_rows.shape[0], key_values.shape[2]
    cap = 3 * rows * routes.shape[1] // 32
    ff = expert_down.shape[1]
    vmem = pl.BlockSpec(memory_space=pltpu.VMEM)
    smem = pl.BlockSpec(memory_space=pltpu.SMEM)
    hbm = pl.BlockSpec(memory_space=pl.ANY)
    most = max(len(b) for b in BATCHES)
    attended, decode_attended, projection = pl.pallas_call(
        attention_kernel,
        out_shape=(
            jax.ShapeDtypeStruct((tokens // 2, 2 * HEAD_DIM), BF16),
            jax.ShapeDtypeStruct((8, HEAD_DIM), BF16),
            jax.ShapeDtypeStruct((HEAD_DIM, width), BF16),
        ),
        in_specs=[hbm, vmem, hbm, smem, vmem, hbm, hbm],
        out_specs=(vmem, vmem, hbm),
        scratch_shapes=[
            pltpu.VMEM((rows, width), BF16),
            pltpu.VMEM((2, tokens // 2, hw), BF16),
            pltpu.VMEM((2, 3, width, HEAD_DIM), BF16),
            pltpu.VMEM((2, count, span, HEAD_DIM), BF16),
            pltpu.VMEM((2, 3, tokens // 2, HEAD_DIM), BF16),
            pltpu.VMEM((8, width), F32),
            pltpu.VMEM((2, 24, HEAD_DIM), F32),
            pltpu.VMEM((4, 24, HEAD_DIM), F32),
            pltpu.SemaphoreType.DMA((44,)),
            pltpu.SemaphoreType.DMA((44,)),
            pltpu.SemaphoreType.DMA((3,)),
        ],
        compiler_params=pltpu.CompilerParams(
            collective_id=0, has_side_effects=True, vmem_limit_bytes=67043328
        ),
        name="attend",
    )(
        prefill_rows,
        decode_rows,
        key_values,
        cache_length,
        attention_gain.reshape(1, width),
        jnp.transpose(query_key_value, (1, 0, 2)),
        out_projection,
    )
    results = pl.pallas_call(
        layer_kernel,
        out_shape=(
            jax.ShapeDtypeStruct((rows, width), BF16),
            jax.ShapeDtypeStruct((count, width), BF16),
        ),
        in_specs=[hbm, vmem, hbm, vmem, vmem, hbm, hbm, vmem, vmem] + [smem] * 2 + [vmem] + [hbm] * 4,
        out_specs=(vmem, vmem),
        scratch_shapes=[
            pltpu.VMEM((rows, width), BF16),
            pltpu.VMEM((tokens // 2, 2 * HEAD_DIM), BF16),
            pltpu.VMEM((2 * HEAD_DIM, width), BF16),
            pltpu.VMEM((2, tokens + 16, hw), BF16),
            pltpu.VMEM((2, 16, rows, hw), BF16),
            pltpu.VMEM((2, 5, 2, rows // 2, hw), BF16),
            pltpu.VMEM((2, 5, 2, rows, hw), BF16),
            pltpu.VMEM((width, 2 * ff), BF16),
            pltpu.VMEM((ff, width), BF16),
            pltpu.VMEM((768, width), BF16),
            pltpu.VMEM((384, width), BF16),
            pltpu.VMEM((most * cap + 16, width), BF16),
            pltpu.VMEM((most * cap + 16, ff), BF16),
            pltpu.VMEM((most * cap + 16, width), BF16),
            pltpu.VMEM((most * rows + 16, 384), BF16),
            pltpu.VMEM((most * rows + 16, 128), F32),
            pltpu.VMEM((16, cap, 128), F32),
            pltpu.VMEM((16, cap, rows), BF16),
            pltpu.VMEM((16, rows, rows), BF16),
            pltpu.VMEM((4, 4, 16, rows), BF16),
            pltpu.VMEM((8, width), F32),
            pltpu.VMEM((4, 8, width), BF16),
            pltpu.VMEM((4, 3, 8, width), BF16),
            pltpu.VMEM((rows, width), BF16),
            pltpu.SemaphoreType.DMA((138,)),
            pltpu.SemaphoreType.DMA((138,)),
            pltpu.SemaphoreType.DMA((13,)),
        ],
        compiler_params=pltpu.CompilerParams(
            collective_id=1, has_side_effects=True, vmem_limit_bytes=67043328
        ),
        name="layer",
    )(
        prefill_rows,
        decode_rows,
        attended,
        decode_attended,
        feedforward_gain.reshape(1, width),
        out_projection,
        projection,
        routes.T,
        route_weight.T,
        decode_routes,
        decode_weight,
        shared_gate.reshape(1, width),
        expert_gate_up[0],
        expert_down[0],
        jnp.transpose(shared_gate_up, (1, 2, 0)),
        shared_down,
    )
    return pl.pallas_call(
        write_kernel,
        out_shape=tuple(jax.ShapeDtypeStruct(r.shape, r.dtype) for r in results),
        in_specs=[vmem, vmem],
        out_specs=(vmem, vmem),
        name="write",
    )(*results)


def solution(mesh):
    return jax.shard_map(
        per_device,
        mesh=mesh,
        in_specs=(
            P(("blk", "expert"), None),
            P(),
            P(None, None, "blk", "expert"),
            P(),
            P(),
            P(),
            P(None, None, "expert"),
            P("expert", None),
            P(("blk", "expert"), None),
            P(("blk", "expert"), None),
            P(),
            P(),
            P("expert", None, None),
            P("expert", None, None),
            P(None, None, "expert"),
            P("expert", None),
            P(),
        ),
        out_specs=(P(("blk", "expert"), None), P()),
        check_vma=False,
    )
```

```python
import math

import jax
import jax.numpy as jnp
from jax import lax
from jax.experimental import pallas as pl
from jax.experimental.pallas import tpu as pltpu
from jax.sharding import PartitionSpec as P

HEAD_DIM = 128
REQUEST_LEN = 1024
EPS = 1e-06
MESH = pl.DeviceIdType.MESH
F32 = jnp.float32
BF16 = jnp.bfloat16

BATCHES = (
    ((0, 0), (0, 1), (0, 3), (1, 0), (3, 0)),
    ((1, 1), (1, 3), (3, 1), (3, 3), (2, 0), (0, 2)),
    ((1, 2), (2, 1)),
    ((3, 2), (2, 3), (2, 2)),
)
SLOT = {place: at for at, place in enumerate(sum(BATCHES, ()))}
STARTS = (0, 5, 11, 13)
PAIR_BATCHES = (((0, 0), (0, 1), (0, 3), (1, 0)), ((0, 2), (1, 1), (1, 3), (1, 2)))
PAIR = {place: at for at, place in enumerate(sum(PAIR_BATCHES, ()))}


def nn(a, b):
    return lax.dot_general(a, b, (((1,), (0,)), ((), ())), preferred_element_type=F32)


def nt(a, b):
    return lax.dot_general(a, b, (((1,), (1,)), ((), ())), preferred_element_type=F32)


def normed(values, gain):
    factor = lax.rsqrt(jnp.mean(values * values, axis=-1, keepdims=True) + EPS)
    return (values * factor * gain).astype(BF16)


def silu(v):
    return v * (1.0 / (1.0 + jnp.exp(-v)))


class Place:
    def __init__(self):
        self.b = lax.axis_index("blk")
        self.e = lax.axis_index("expert")
        self.x = self.e // 4
        self.z = self.e % 4

        odd = self.x % 2
        self.mate = lambda: self.at(1 + 2 * odd, 0)
        self.other = lambda: self.at(3 - 2 * odd, 0)
        self.odd = odd

    def at(self, dx, dz):
        return (self.b, ((self.x + dx) % 4) * 4 + (self.z + dz) % 4)

    def block(self, place):
        half = self.odd if place[0] == 0 else 1 - self.odd
        return half * 4 + (self.z + place[1]) % 4


def greet(peers):
    barrier = pltpu.get_barrier_semaphore()
    for peer in peers:
        pl.semaphore_signal(barrier, inc=1, device_id=peer, device_id_type=MESH)
    return lambda: pl.semaphore_wait(barrier, len(peers))


def remote(src, dst, send, recv, at, device):
    return pltpu.make_async_remote_copy(
        src_ref=src,
        dst_ref=dst,
        send_sem=send.at[at],
        recv_sem=recv.at[at],
        device_id=device,
        device_id_type=MESH,
    )


def slot(half, p, q):
    return SLOT[(p, q) if half == 0 else (q, p)]


def sides(here, half):
    along_x = (here.at(1, 0), here.at(3, 0))
    along_z = (here.at(0, 1), here.at(0, 3))
    return along_x + along_z if half == 0 else along_z + along_x


class Gather:
    def __init__(self, here, rows_ref, rows, send, recv, base):
        self.copies = []
        hr = rows // 2
        for half in range(2):
            major_p, major_m, minor_p, minor_m = sides(here, half)
            c = {}

            def put(name, at, src, dst, part, device):
                lo, size = part
                c[name] = remote(
                    rows_ref.at[half, pl.ds(slot(half, *src) * rows + lo, size)],
                    rows_ref.at[half, pl.ds(slot(half, *dst) * rows + lo, size)],
                    send,
                    recv,
                    base + half * 20 + at,
                    device,
                )

            whole, low, high = (0, rows), (0, hr), (hr, hr)
            put("n+", 0, (0, 0), (0, 3), whole, minor_p)
            put("n-", 1, (0, 0), (0, 1), whole, minor_m)
            put("fn+", 4, (0, 3), (0, 2), high, minor_p)
            put("fn-", 5, (0, 1), (0, 2), low, minor_m)
            for q, at in ((0, 2), (1, 6), (3, 8), (2, 10)):
                put(("j+", q), at, (0, q), (3, q), whole, major_p)
                put(("j-", q), at + 1, (0, q), (1, q), whole, major_m)
            for q, at in ((0, 12), (1, 14), (3, 16), (2, 18)):
                put(("f+", q), at, (3, q), (2, q), high, major_p)
                put(("f-", q), at + 1, (1, q), (2, q), low, major_m)
            self.copies.append(c)

    def start(self, *names):
        for c in self.copies:
            for name in names:
                c[name].start()

    def got(self, *names):
        for c in self.copies:
            for name in names:
                c[name].wait_recv()

    def open(self):
        self.start("n+", "n-", ("j+", 0), ("j-", 0))

    def to_batch_0(self):
        self.got("n+", "n-")
        self.start("fn+", "fn-", ("j+", 1), ("j-", 1), ("j+", 3), ("j-", 3))
        self.got(("j+", 0), ("j-", 0))
        self.start(("f+", 0), ("f-", 0))

    def to_batch_1(self):
        self.got("fn+", "fn-")
        self.start(("j+", 2), ("j-", 2))
        self.got(("j+", 1), ("j-", 1))
        self.start(("f+", 1), ("f-", 1))
        self.got(("j+", 3), ("j-", 3))
        self.start(("f+", 3), ("f-", 3))
        self.got(("f+", 0), ("f-", 0))

    def to_batch_2(self):
        self.got(("j+", 2), ("j-", 2))
        self.start(("f+", 2), ("f-", 2))
        self.got(("f+", 1), ("f-", 1))

    def to_batch_3(self):
        for q in (3, 2):
            self.got(("f+", q), ("f-", q))

    def close(self):
        for c in self.copies:
            for copy in c.values():
                copy.wait_send()


class PairGather:
    def __init__(self, here, rows_ref, rows, send, recv):
        hr = rows // 2
        self.c = c = {}
        z_p, z_m, mate = here.at(0, 1), here.at(0, 3), here.mate()

        def put(name, half, src, dst, lo, size, device):
            c[name] = remote(
                rows_ref.at[half, pl.ds(PAIR[src] * rows + lo, size)],
                rows_ref.at[half, pl.ds(PAIR[dst] * rows + lo, size)],
                send,
                recv,
                len(c),
                device,
            )

        for half, a in ((0, 0), (1, 0), (1, 1)):
            put(("+", half, a), half, (a, 0), (a, 3), 0, rows, z_p)
            put(("-", half, a), half, (a, 0), (a, 1), 0, rows, z_m)
            put(("f+", half, a), half, (a, 3), (a, 2), hr, hr, z_p)
            put(("f-", half, a), half, (a, 1), (a, 2), 0, hr, z_m)
        for q in (0, 1, 3, 2):
            put(("m", 0, q), 0, (0, q), (1, q), 0, rows, mate)
        put(("m", 1, 0), 1, (0, 0), (1, 0), 0, rows, mate)

    def start(self, *names):
        for name in names:
            self.c[name].start()

    def got(self, *names):
        for name in names:
            self.c[name].wait_recv()

    def open(self):
        self.start(("+", 0, 0), ("-", 0, 0), ("m", 1, 0), ("m", 0, 0), ("+", 1, 0), ("-", 1, 0))

    def to_batch_0(self):
        self.got(("+", 0, 0), ("-", 0, 0))
        self.start(("f+", 0, 0), ("f-", 0, 0), ("m", 0, 1), ("m", 0, 3))
        self.got(("m", 1, 0))
        self.start(("+", 1, 1), ("-", 1, 1))
        self.got(("+", 1, 0), ("-", 1, 0))
        self.start(("f+", 1, 0), ("f-", 1, 0))
        self.got(("m", 0, 0))

    def relay(self):
        self.got(("f+", 0, 0), ("f-", 0, 0))
        self.start(("m", 0, 2))
        self.got(("+", 1, 1), ("-", 1, 1))
        self.start(("f+", 1, 1), ("f-", 1, 1))

    def to_batch_1(self):
        self.got(("m", 0, 1), ("m", 0, 3), ("m", 0, 2))
        self.got(("f+", 1, 0), ("f-", 1, 0), ("f+", 1, 1), ("f-", 1, 1))

    def close(self):
        for copy in self.c.values():
            copy.wait_send()


class PairScatter:
    def __init__(self, here, part_ref, fwd_ref, full_ref, send, recv):
        self.part, self.fwd, self.full = part_ref, fwd_ref, full_ref
        self.c = c = {}
        rows = part_ref.shape[2]
        hr = rows // 2
        self.low, self.high = pl.ds(0, hr), pl.ds(hr, hr)
        z_p, z_m, mate = here.at(0, 1), here.at(0, 3), here.mate()

        def put(name, src, dst, device):
            c[name] = remote(src, dst, send, recv, len(c), device)

        for half, a, k in ((0, 0, 4), (1, 1, 1), (1, 0, 0)):
            far, plus, minus = PAIR[a, 2], PAIR[a, 1], PAIR[a, 3]
            put(("f+", half, a), part_ref.at[half, far, self.low], fwd_ref.at[half, k, 0], z_p)
            put(("f-", half, a), part_ref.at[half, far, self.high], fwd_ref.at[half, k, 1], z_m)
            put(("t+", half, a), part_ref.at[half, plus], full_ref.at[half, k, 0], z_p)
            put(("t-", half, a), part_ref.at[half, minus], full_ref.at[half, k, 1], z_m)
        for q in range(4):
            put(("m", 0, q), part_ref.at[0, PAIR[1, q]], full_ref.at[0, q, 0], mate)
        put(("m", 1, 0), part_ref.at[1, PAIR[1, 0]], full_ref.at[1, 4, 0], mate)
        self.slots = {(0, 0): 4, (1, 1): 1, (1, 0): 0}

    def start(self, *names):
        for name in names:
            self.c[name].start()

    def far(self, half, a):
        self.start(("f+", half, a), ("f-", half, a))

    def pass_plus(self, half, a):
        self.c["f+", half, a].wait_recv()
        at, k = PAIR[a, 1], self.slots[half, a]
        self.part[half, at, self.low] = (
            self.part[half, at, self.low].astype(F32) + self.fwd[half, k, 0].astype(F32)
        ).astype(BF16)
        self.c["t+", half, a].start()

    def pass_minus(self, half, a):
        self.c["f-", half, a].wait_recv()
        at, k = PAIR[a, 3], self.slots[half, a]
        self.part[half, at, self.high] = (
            self.part[half, at, self.high].astype(F32) + self.fwd[half, k, 1].astype(F32)
        ).astype(BF16)
        self.c["t-", half, a].start()

    def ring(self, half, a):
        self.c["t+", half, a].wait_recv()
        self.c["t-", half, a].wait_recv()
        k = self.slots[half, a]
        return (
            self.part[half, PAIR[a, 0]].astype(F32)
            + self.full[half, k, 0].astype(F32)
            + self.full[half, k, 1].astype(F32)
        )

    def meet(self, q):
        self.c["m", 0, q].wait_recv()
        at = PAIR[0, q]
        self.part[0, at] = (self.part[0, at].astype(F32) + self.full[0, q, 0].astype(F32)).astype(BF16)

    def finish(self):
        self.meet(2)
        self.far(0, 0)
        self.meet(1)
        self.pass_plus(0, 0)
        self.meet(3)
        self.pass_minus(0, 0)
        self.part[1, PAIR[1, 0]] = self.ring(1, 1).astype(BF16)
        self.start(("m", 1, 0))
        self.meet(0)
        right = self.ring(1, 0)
        left = self.ring(0, 0)
        self.c["m", 1, 0].wait_recv()
        return [left, right + self.full[1, 4, 0].astype(F32)]

    def close(self):
        for copy in self.c.values():
            copy.wait_send()


class Scatter:
    def __init__(self, here, part_ref, fwd_ref, full_ref, send, recv, base):
        self.part, self.fwd, self.full = part_ref, fwd_ref, full_ref
        self.copies = []
        rows = part_ref.shape[2]
        hr = rows // 2
        self.low, self.high = pl.ds(0, hr), pl.ds(hr, hr)
        for half in range(2):
            major_p, major_m, minor_p, minor_m = sides(here, half)
            c = {}

            def put(q, far, plus, minus, side_p, side_m):
                at = base + half * 20 + 4 * q
                c["f+", q] = remote(
                    part_ref.at[half, far, self.low], fwd_ref.at[half, q, 0], send, recv, at, side_p
                )
                c["f-", q] = remote(
                    part_ref.at[half, far, self.high], fwd_ref.at[half, q, 1], send, recv, at + 1, side_m
                )
                c["t+", q] = remote(
                    part_ref.at[half, plus], full_ref.at[half, q, 0], send, recv, at + 2, side_p
                )
                c["t-", q] = remote(
                    part_ref.at[half, minus], full_ref.at[half, q, 1], send, recv, at + 3, side_m
                )

            for q in range(4):
                put(q, slot(half, 2, q), slot(half, 1, q), slot(half, 3, q), major_p, major_m)
            put(4, slot(half, 0, 2), slot(half, 0, 1), slot(half, 0, 3), minor_p, minor_m)
            self.copies.append(c)

    def _next(self, half, q, p):
        return slot(half, p, q) if q < 4 else slot(half, 0, p)

    def send_far(self, *qs):
        for q in qs:
            for half in range(2):
                self.copies[half]["f+", q].start()
                self.copies[half]["f-", q].start()

    def pass_plus(self, half, q):
        c = self.copies[half]
        c["f+", q].wait_recv()
        at = self._next(half, q, 1)
        self.part[half, at, self.low] = (
            self.part[half, at, self.low].astype(F32) + self.fwd[half, q, 0].astype(F32)
        ).astype(BF16)
        c["t+", q].start()

    def pass_minus(self, half, q):
        c = self.copies[half]
        c["f-", q].wait_recv()
        at = self._next(half, q, 3)
        self.part[half, at, self.high] = (
            self.part[half, at, self.high].astype(F32) + self.fwd[half, q, 1].astype(F32)
        ).astype(BF16)
        c["t-", q].start()

    def pass_on(self, *qs):
        for q in qs:
            for half in range(2):
                self.pass_plus(half, q)
                self.pass_minus(half, q)

    def total(self, half, q):
        c = self.copies[half]
        c["t+", q].wait_recv()
        c["t-", q].wait_recv()
        at = self._next(half, q, 0)
        return (
            self.part[half, at].astype(F32)
            + self.full[half, q, 0].astype(F32)
            + self.full[half, q, 1].astype(F32)
        )

    def line(self, q):
        for half in range(2):
            self.part[half, slot(half, 0, q)] = self.total(half, q).astype(BF16)

    def finish(self, between):
        self.line(2)
        self.send_far(4)
        between()
        self.line(1)
        for half in range(2):
            self.pass_plus(half, 4)
        self.line(3)
        for half in range(2):
            self.pass_minus(half, 4)
        self.line(0)
        return [self.total(half, 4) for half in range(2)]

    def close(self):
        for c in self.copies:
            for copy in c.values():
                copy.wait_send()


def padded_rows(ref, scratch):
    scratch[...] = jnp.zeros_like(scratch)
    scratch[0 : ref.shape[0], :] = ref[...].astype(F32)
    return scratch[...]


def attention_kernel(
    rows_hbm,
    dec_ref,
    cache_hbm,
    length_ref,
    gain_ref,
    qkv_hbm,
    wo_hbm,
    att_ref,
    dec_att_ref,
    other_wo,
    rows_ref,
    g,
    wqkv,
    cache,
    heads,
    dec8,
    dec_out,
    dec_in,
    send,
    recv,
    local_sem,
):
    here = Place()
    rows, width = rows_ref.shape
    hw = width // 2
    blk_count = lax.axis_size("blk")
    score_scale = 1.0 / math.sqrt(HEAD_DIM)
    w_copy = pltpu.make_async_copy(qkv_hbm, wqkv.at[0], local_sem.at[0])
    r_copy = pltpu.make_async_copy(rows_hbm, rows_ref, local_sem.at[2])
    r_copy.start()
    c_copy = pltpu.make_async_copy(cache_hbm, cache, local_sem.at[1])
    w_copy.start()
    c_copy.start()
    core, y = here.b % 2, here.b // 2
    blk_peers = []
    if blk_count > 1:
        blk_peers = [(here.b + 1 - 2 * core, here.e)]
        blk_peers += [(((y + k) % 4) * 2 + core, here.e) for k in (1, 3, 2)]
    wait_all = greet([here.mate(), here.other(), here.at(0, 1), here.at(0, 3)] + blk_peers)
    r_copy.wait()
    own = normed(rows_ref[...].astype(F32), gain_ref[...])
    g[0, 0:rows] = own[:, :hw]
    g[1, 0:rows] = own[:, hw:]
    wait_all()
    gather = PairGather(here, g, rows, send, recv)
    gather.open()
    w_half = pl.ds(pl.multiple_of(core * hw, hw), hw)
    o_half = pl.ds(pl.multiple_of(core * (HEAD_DIM // 2), HEAD_DIM // 2), HEAD_DIM // 2)
    fetch, share = [], []
    if blk_count > 1:
        for i, (src, dst) in enumerate(
            ((qkv_hbm.at[:, w_half], wqkv.at[1, :, w_half]), (wo_hbm.at[o_half], other_wo.at[o_half]))
        ):
            fetch.append(remote(src, dst, send, recv, 36 + i, here.other()))
            share.append(remote(dst, dst, send, recv, 38 + i, blk_peers[0]))
    else:
        for i, (src, dst) in enumerate(
            ((qkv_hbm, wqkv.at[1]), (wo_hbm, other_wo))
        ):
            fetch.append(remote(src, dst, send, recv, 36 + i, here.other()))
    for copy in fetch:
        copy.start()

    dn = normed(padded_rows(dec_ref, dec8), gain_ref[...])
    w_copy.wait()
    q8 = nn(dn, wqkv[0, 0]).astype(BF16)
    k8 = nn(dn, wqkv[0, 1]).astype(BF16)
    v8 = nn(dn, wqkv[0, 2]).astype(BF16)
    c_copy.wait()
    count = cache.shape[1]
    span = cache.shape[2]
    row = lax.broadcasted_iota(jnp.int32, (8, 1), 0)
    scores = jnp.zeros((8, span), F32)
    lengths = jnp.zeros((8, 1), jnp.int32)
    for d in range(count):
        scores = jnp.where(row == d, nt(q8, cache[0, d]), scores)
        lengths = jnp.where(row == d, length_ref[d], lengths)
    position = here.b * span + lax.broadcasted_iota(jnp.int32, (8, span), 1)
    valid = position < lengths
    masked = jnp.where(valid, scores * score_scale, -1e30)
    top = jnp.max(masked, axis=-1, keepdims=True)
    weights = jnp.where(valid, jnp.exp(masked - top), 0.0)
    total = jnp.sum(weights, axis=-1, keepdims=True)
    coarse = weights.astype(BF16).astype(F32)
    both = jnp.concatenate([coarse, weights - coarse], axis=0).astype(BF16)
    mix = jnp.zeros((8, HEAD_DIM), F32)
    for d in range(count):
        pair = nn(both, cache[1, d])
        mix = jnp.where(row == d, pair[0:8] + pair[8:16], mix)

    def pack(at, mix, top, total):
        dec_out[at, 0:8] = mix
        dec_out[at, 8:16] = jnp.broadcast_to(top, (8, HEAD_DIM))
        dec_out[at, 16:24] = jnp.broadcast_to(total, (8, HEAD_DIM))

    def merge(mix, top, total, at):
        other_top = dec_in[at, 8:16]
        new_top = jnp.maximum(top, other_top)
        mine, theirs = jnp.exp(top - new_top), jnp.exp(other_top - new_top)
        return (
            mix * mine + dec_in[at, 0:8] * theirs,
            new_top,
            total * mine + dec_in[at, 16:24] * theirs,
        )

    top = jnp.broadcast_to(top, (8, HEAD_DIM))
    total = jnp.broadcast_to(total, (8, HEAD_DIM))
    pack(0, mix, top, total)
    blk_copies = [
        remote(dec_out.at[min(k, 1)], dec_in.at[k], send, recv, 40 + k, peer)
        for k, peer in enumerate(blk_peers)
    ]
    for copy in blk_copies[:1]:
        copy.start()

    def project(batch, head):
        n = len(PAIR_BATCHES[batch])
        lo, size = batch * n * rows, n * rows
        left, right = g[0, lo : lo + size], g[1, lo : lo + size]
        for which in range(3):
            w = wqkv.at[head, which]
            out = (nn(left, w[0:hw]) + nn(right, w[hw:width])).astype(BF16)
            for j, place in enumerate(PAIR_BATCHES[batch]):
                at = pl.multiple_of(here.block(place) * rows, rows)
                heads[head, which, pl.ds(at, rows)] = out[j * rows : (j + 1) * rows]

    gather.to_batch_0()
    project(0, 0)
    gather.relay()
    for copy in fetch:
        copy.wait_recv()
    for copy in share:
        copy.start()
    if blk_copies:
        blk_copies[0].wait_recv()
        mix, top, total = merge(mix, top, total, 0)
        pack(1, mix, top, total)
        for copy in blk_copies[1:]:
            copy.start()
    for copy in share:
        copy.wait_recv()
    project(0, 1)
    gather.to_batch_1()
    project(1, 0)
    project(1, 1)
    for k, copy in enumerate(blk_copies[1:]):
        copy.wait_recv()
        mix, top, total = merge(mix, top, total, k + 1)
    q32, k32, v32 = q8.astype(F32), k8.astype(F32), v8.astype(F32)
    new_score = jnp.sum(q32 * k32, axis=-1, keepdims=True) * score_scale
    new_top = jnp.maximum(top, new_score)
    old = jnp.exp(top - new_top)
    fresh = jnp.exp(new_score - new_top)
    dec_att_ref[...] = ((mix * old + fresh * v32) / (total * old + fresh)).astype(BF16)

    step = 256
    diagonal = lax.broadcasted_iota(jnp.int32, (step, step), 0) >= lax.broadcasted_iota(
        jnp.int32, (step, step), 1
    )

    def one_head(head, carry):
        lanes = pl.ds(pl.multiple_of(head * HEAD_DIM, HEAD_DIM), HEAD_DIM)
        for qb in range(REQUEST_LEN // step):
            at = qb * step
            q = heads[head, 0, at : at + step]
            s1 = jnp.where(diagonal, nt(q, heads[head, 1, at : at + step]) * score_scale, -jnp.inf)
            top_q = jnp.max(s1, axis=-1, keepdims=True)
            if qb:
                s0 = nt(q, heads[head, 1, 0:at]) * score_scale
                top_q = jnp.maximum(top_q, jnp.max(s0, axis=-1, keepdims=True))
            p1 = jnp.exp(s1 - top_q)
            sum_q = jnp.sum(p1, axis=-1, keepdims=True)
            out = nn(p1.astype(BF16), heads[head, 2, at : at + step])
            if qb:
                p0 = jnp.exp(s0 - top_q)
                sum_q = sum_q + jnp.sum(p0, axis=-1, keepdims=True)
                out = out + nn(p0.astype(BF16), heads[head, 2, 0:at])
            att_ref[at : at + step, lanes] = (out / sum_q).astype(BF16)
        return carry

    lax.fori_loop(0, 2, one_head, 0)
    for copy in fetch + share:
        copy.wait_send()
    gather.close()
    for copy in blk_copies:
        copy.wait_send()


def layer_kernel(
    rows_hbm,
    dec_ref,
    att_hbm,
    dec_att_ref,
    gain_ref,
    own_wo,
    other_wo,
    routes_ref,
    weight_ref,
    dec_routes_ref,
    dec_weight_ref,
    gate_ref,
    wgu_hbm,
    wd_hbm,
    wst_hbm,
    wsd_hbm,
    out_ref,
    dec_out_ref,
    rows_ref,
    att_ref,
    wo_ref,
    g,
    part,
    fwd,
    full,
    wgu,
    wd,
    wsp,
    wsd,
    xe,
    he,
    ye,
    hs,
    gv,
    wslot,
    pick,
    back,
    meta,
    dec8,
    dec_send,
    dec_recv,
    res,
    send,
    recv,
    local_sem,
):
    here = Place()
    early = [
        pltpu.make_async_copy(a, b, local_sem.at[9 + i])
        for i, (a, b) in enumerate(
            (
                (att_hbm, att_ref),
                (own_wo, wo_ref.at[pl.ds(0, HEAD_DIM)]),
                (other_wo, wo_ref.at[pl.ds(HEAD_DIM, HEAD_DIM)]),
                (rows_hbm, rows_ref),
            )
        )
    ]
    for copy in early:
        copy.start()
    rows, width = rows_ref.shape
    hw = width // 2
    cap = pick.shape[1]
    ff = wd.shape[0]
    sff = wsd_hbm.shape[0]
    count = dec_ref.shape[0]
    tail = sff - 256
    tile = min(256, hw)

    moves = [(wgu_hbm, wgu), (wd_hbm, wd), (wsd_hbm, wsd.at[pl.ds(0, sff)])]
    for group, size in enumerate((128, 128, tail)):
        for kind in range(2):
            moves.append(
                (
                    wst_hbm.at[kind, pl.ds(group * 128, size)],
                    wsp.at[pl.ds(group * 256 + kind * 128, size)],
                )
            )
    local = [pltpu.make_async_copy(a, b, local_sem.at[i]) for i, (a, b) in enumerate(moves)]
    peers = [here.at(1, 0), here.at(3, 0), here.at(0, 1), here.at(0, 3), here.at(2, 0), here.at(0, 2)]
    wait_all = greet(peers)

    weight = weight_ref[...]
    coarse = weight.astype(BF16).astype(F32)
    meta[0, 0] = jnp.concatenate(
        [routes_ref[...].astype(F32), coarse, weight - coarse, jnp.zeros_like(weight)], axis=0
    ).astype(BF16)

    def out_project(*places):
        for place in places:
            at = pl.multiple_of(here.block(place) * rows, rows)
            term = nn(att_ref[pl.ds(at, rows)], wo_ref[...]).astype(BF16)
            part[0, PAIR[place]] = term[:, :hw]
            part[1, PAIR[place]] = term[:, hw:]

    first = PairScatter(here, part, fwd, full, send, recv)
    gather = Gather(here, g, rows, send, recv, 40)
    second = Scatter(here, part, fwd, full, send, recv, 80)

    def exchange(buf_send, buf_recv, base, along):
        steps = ((1, 0), (3, 0), (2, 0)) if along == 0 else ((0, 1), (0, 3), (0, 2))
        return [
            remote(buf_send, buf_recv.at[k], send, recv, base + k, here.at(*step))
            for k, step in enumerate(steps)
        ]

    meta_z = [
        remote(meta.at[0, 0], meta.at[0, dst], send, recv, 120 + k, here.at(0, dz))
        for k, (dz, dst) in enumerate(((1, 3), (3, 1), (2, 2)))
    ]
    meta_x = [
        remote(meta.at[0], meta.at[dst], send, recv, 123 + k, here.at(dx, 0))
        for k, (dx, dst) in enumerate(((1, 3), (3, 1), (2, 2)))
    ]
    dec_copies = [
        exchange(dec_send.at[k], dec_recv.at[k], 126 + 3 * k, 1 - k % 2) for k in range(4)
    ]

    for copy in early:
        copy.wait()
    out_project((1, 2))
    dec_term = nn(dec_att_ref[...], wo_ref[0:HEAD_DIM])
    dec_send[0] = dec_term.astype(BF16)
    wait_all()
    for copy in meta_z + dec_copies[0]:
        copy.start()
    first.start(("m", 0, 2))
    first.far(1, 1)
    for copy in local:
        copy.start()
    out_project((1, 1))
    first.start(("m", 0, 1))
    out_project((0, 2))
    first.far(1, 0)
    out_project((1, 3))
    first.start(("m", 0, 3))
    first.pass_plus(1, 1)
    first.pass_minus(1, 1)
    out_project((1, 0))
    first.start(("m", 0, 0))
    out_project((0, 1), (0, 3))
    first.pass_plus(1, 0)
    first.pass_minus(1, 0)
    out_project((0, 0))

    def dec_sum(k):
        total = dec_send[k].astype(F32)
        for copy in dec_copies[k]:
            copy.wait_recv()
        for at in range(3):
            total = total + dec_recv[k, at].astype(F32)
        return total

    for copy in meta_z:
        copy.wait_recv()
    for copy in meta_x:
        copy.start()
    dec_send[1] = dec_sum(0).astype(BF16)
    for copy in dec_copies[1]:
        copy.start()

    halves = first.finish()
    sum_sq = jnp.zeros((rows, 1), F32)
    for half in range(2):
        cols = pl.ds(half * hw, hw)
        value = (rows_ref[:, cols].astype(F32) + halves[half]).astype(BF16)
        res[:, cols] = value
        wide = value.astype(F32)
        sum_sq = sum_sq + jnp.sum(wide * wide, axis=-1, keepdims=True)
    factor = lax.rsqrt(sum_sq / width + EPS)
    for half in range(2):
        cols = pl.ds(half * hw, hw)
        g[half, 0:rows] = (res[:, cols].astype(F32) * factor * gain_ref[:, cols]).astype(BF16)
    gather.open()

    gate = gate_ref[...]
    gate_coarse = gate.astype(BF16).astype(F32)
    for copy in local:
        copy.wait()
    pad = 128 - tail
    row_at = lax.broadcasted_iota(jnp.int32, (pad, width), 0)
    wsp[512 + tail : 640] = jnp.where(
        row_at == 0, gate_coarse, jnp.where(row_at == 1, gate - gate_coarse, 0.0)
    ).astype(BF16)
    wsp[640 + tail : 768] = jnp.zeros((pad, width), BF16)
    wsd[sff : wsd.shape[0]] = jnp.zeros((wsd.shape[0] - sff, width), BF16)

    for copy in meta_x:
        copy.wait_recv()
    expert = here.e.astype(F32)
    iota_r = lax.broadcasted_iota(jnp.int32, (rows, rows), 0)
    iota_c = lax.broadcasted_iota(jnp.int32, (rows, rows), 1)
    upper = (iota_r <= iota_c).astype(F32).astype(BF16)
    eye = (iota_r == iota_c).astype(F32).astype(BF16)
    iota_cap = lax.broadcasted_iota(jnp.int32, (cap, rows), 0).astype(F32)
    iota_lane = iota_c.astype(F32)
    chosen, scales = [], []
    for place in SLOT:
        info = meta[place[0], place[1]].astype(F32)
        match = info[0:4] == expert
        chosen.append(jnp.sum(match.astype(F32), axis=0, keepdims=True))
        scales.append(jnp.sum(jnp.where(match, info[4:8] + info[8:12], 0.0), axis=0, keepdims=True))
    chosen = jnp.concatenate(chosen, axis=0)
    order = nn(chosen.astype(BF16), upper) - 1.0
    order = jnp.where(chosen > 0.0, order, -1.0)
    columns = nt(eye, order.astype(BF16))
    for at in range(16):
        choice = iota_cap == order[at : at + 1]
        pick[at] = choice.astype(F32).astype(BF16)
        wslot[at] = jnp.broadcast_to(
            jnp.sum(jnp.where(choice, scales[at], 0.0), axis=1, keepdims=True), (cap, 128)
        )
        back[at] = (iota_lane == columns[:, at : at + 1]).astype(F32).astype(BF16)

    dec_res = (padded_rows(dec_ref, dec8) + dec_sum(1)).astype(BF16).astype(F32)
    dec_two = normed(dec_res, gain_ref[...])
    dec8[...] = dec_res
    base_row = 16 * rows
    dec_pad = jnp.concatenate([dec_two.astype(F32), jnp.zeros((8, width), F32)], axis=0).astype(BF16)
    g[0, base_row : base_row + 16] = dec_pad[:, :hw]
    g[1, base_row : base_row + 16] = dec_pad[:, hw:]

    first.close()

    row8 = lax.broadcasted_iota(jnp.int32, (16, 1), 0)
    dec_scale = jnp.zeros((16, 1), F32)
    for d in range(count):
        one = jnp.float32(0.0)
        for k in range(dec_routes_ref.shape[1]):
            one = one + jnp.where(dec_routes_ref[d, k] == here.e, dec_weight_ref[d, k], 0.0)
        dec_scale = jnp.where(row8 == d, one, dec_scale)

    def feed_forward(batch):
        places = BATCHES[batch]
        start, n = STARTS[batch], len(places)
        decode = batch == 3
        extra = 16 if decode else 0
        m, me = n * rows + extra, n * cap + extra
        lo = start * rows
        for j in range(n):
            at = lo + j * rows
            for half in range(2):
                xe[j * cap : (j + 1) * cap, half * hw : (half + 1) * hw] = nn(
                    pick[start + j], g[half, at : at + rows]
                ).astype(BF16)
        if decode:
            xe[n * cap : me] = dec_pad

        def up(i, carry):
            at = pl.multiple_of(i * 128, 128)
            w = jnp.concatenate([wgu[:, pl.ds(at, 128)], wgu[:, pl.ds(ff + at, 128)]], axis=1)
            hidden = nn(xe[0:me], w)
            he[0:me, pl.ds(at, 128)] = (silu(hidden[:, 0:128]) * hidden[:, 128:256]).astype(BF16)
            return carry

        lax.fori_loop(0, ff // 128, up, 0)

        scale = jnp.concatenate(
            [wslot[start + j][:, 0:1] for j in range(n)] + ([dec_scale] if decode else []), axis=0
        )

        def down(i, carry):
            cols = pl.ds(pl.multiple_of(i * tile, tile), tile)
            ye[0:me, cols] = (nn(he[0:me], wd[:, cols]) * scale).astype(BF16)
            return carry

        lax.fori_loop(0, width // tile, down, 0)

        for group in range(3):
            w = wsp.at[pl.ds(group * 256, 256)]
            hidden = nt(g[0, lo : lo + m], w[:, 0:hw]) + nt(g[1, lo : lo + m], w[:, hw:width])
            hs[0:m, group * 128 : (group + 1) * 128] = (
                silu(hidden[:, 0:128]) * hidden[:, 128:256]
            ).astype(BF16)
            if group == 2:
                logit = hidden[:, tail : tail + 1] + hidden[:, tail + 1 : tail + 2]
                gv[0:m] = jnp.broadcast_to(1.0 / (1.0 + jnp.exp(-logit)), (m, 128))

        for half in range(2):

            def combine(i, carry, half=half):
                here_cols = pl.ds(pl.multiple_of(i * tile, tile), tile)
                cols = pl.ds(pl.multiple_of(half * hw + i * tile, tile), tile)
                shared = nn(hs[0:m], wsd[:, cols]) * gv[0:m, 0:1]
                for j in range(n):
                    routed = nn(back[start + j][:, 0:cap], ye[j * cap : (j + 1) * cap, cols])
                    part[half, start + j, :, here_cols] = (
                        shared[j * rows : (j + 1) * rows] + routed
                    ).astype(BF16)
                if decode:
                    dec_send[2, :, cols] = (
                        shared[n * rows : n * rows + 8] + ye[n * cap : n * cap + 16, cols].astype(F32)[0:8]
                    ).astype(BF16)
                return carry

            lax.fori_loop(0, hw // tile, combine, 0)

    gather.to_batch_0()
    feed_forward(0)
    gather.to_batch_1()
    feed_forward(1)
    gather.to_batch_2()
    second.send_far(0)
    feed_forward(2)
    second.send_far(1)
    second.pass_on(0)
    gather.to_batch_3()
    second.pass_on(1)
    feed_forward(3)
    for copy in dec_copies[2]:
        copy.start()
    second.send_far(2, 3)
    second.pass_on(2, 3)

    def decode_turn():
        dec_send[3] = dec_sum(2).astype(BF16)
        for copy in dec_copies[3]:
            copy.start()

    halves = second.finish(decode_turn)
    for half in range(2):
        cols = pl.ds(half * hw, hw)
        out_ref[:, cols] = (res[:, cols].astype(F32) + halves[half]).astype(BF16)
    dec_out_ref[...] = (dec8[...] + dec_sum(3)).astype(BF16)[0:count]
    gather.close()
    second.close()
    for copy in meta_z + meta_x + sum(dec_copies, []):
        copy.wait_send()


def write_kernel(a_ref, b_ref, a_out, b_out):
    a_out[...] = a_ref[...]
    b_out[...] = b_ref[...]


def per_device(
    prefill_rows,
    decode_rows,
    key_values,
    cache_length,
    attention_gain,
    feedforward_gain,
    query_key_value,
    out_projection,
    routes,
    route_weight,
    decode_routes,
    decode_weight,
    expert_gate_up,
    expert_down,
    shared_gate_up,
    shared_down,
    shared_gate,
):
    rows, width = prefill_rows.shape
    hw = width // 2
    tokens = rows * 16
    count, span = decode_rows.shape[0], key_values.shape[2]
    cap = 3 * rows * routes.shape[1] // 32
    ff = expert_down.shape[1]
    vmem = pl.BlockSpec(memory_space=pltpu.VMEM)
    smem = pl.BlockSpec(memory_space=pltpu.SMEM)
    hbm = pl.BlockSpec(memory_space=pl.ANY)
    most = max(len(b) for b in BATCHES)
    attended, decode_attended, projection = pl.pallas_call(
        attention_kernel,
        out_shape=(
            jax.ShapeDtypeStruct((tokens // 2, 2 * HEAD_DIM), BF16),
            jax.ShapeDtypeStruct((8, HEAD_DIM), BF16),
            jax.ShapeDtypeStruct((HEAD_DIM, width), BF16),
        ),
        in_specs=[hbm, vmem, hbm, smem, vmem, hbm, hbm],
        out_specs=(vmem, vmem, hbm),
        scratch_shapes=[
            pltpu.VMEM((rows, width), BF16),
            pltpu.VMEM((2, tokens // 2, hw), BF16),
            pltpu.VMEM((2, 3, width, HEAD_DIM), BF16),
            pltpu.VMEM((2, count, span, HEAD_DIM), BF16),
            pltpu.VMEM((2, 3, tokens // 2, HEAD_DIM), BF16),
            pltpu.VMEM((8, width), F32),
            pltpu.VMEM((2, 24, HEAD_DIM), F32),
            pltpu.VMEM((4, 24, HEAD_DIM), F32),
            pltpu.SemaphoreType.DMA((44,)),
            pltpu.SemaphoreType.DMA((44,)),
            pltpu.SemaphoreType.DMA((3,)),
        ],
        compiler_params=pltpu.CompilerParams(
            collective_id=0, has_side_effects=True, vmem_limit_bytes=67043328
        ),
        name="attend",
    )(
        prefill_rows,
        decode_rows,
        key_values,
        cache_length,
        attention_gain.reshape(1, width),
        jnp.transpose(query_key_value, (1, 0, 2)),
        out_projection,
    )
    results = pl.pallas_call(
        layer_kernel,
        out_shape=(
            jax.ShapeDtypeStruct((rows, width), BF16),
            jax.ShapeDtypeStruct((count, width), BF16),
        ),
        in_specs=[hbm, vmem, hbm, vmem, vmem, hbm, hbm, vmem, vmem] + [smem] * 2 + [vmem] + [hbm] * 4,
        out_specs=(vmem, vmem),
        scratch_shapes=[
            pltpu.VMEM((rows, width), BF16),
            pltpu.VMEM((tokens // 2, 2 * HEAD_DIM), BF16),
            pltpu.VMEM((2 * HEAD_DIM, width), BF16),
            pltpu.VMEM((2, tokens + 16, hw), BF16),
            pltpu.VMEM((2, 16, rows, hw), BF16),
            pltpu.VMEM((2, 5, 2, rows // 2, hw), BF16),
            pltpu.VMEM((2, 5, 2, rows, hw), BF16),
            pltpu.VMEM((width, 2 * ff), BF16),
            pltpu.VMEM((ff, width), BF16),
            pltpu.VMEM((768, width), BF16),
            pltpu.VMEM((384, width), BF16),
            pltpu.VMEM((most * cap + 16, width), BF16),
            pltpu.VMEM((most * cap + 16, ff), BF16),
            pltpu.VMEM((most * cap + 16, width), BF16),
            pltpu.VMEM((most * rows + 16, 384), BF16),
            pltpu.VMEM((most * rows + 16, 128), F32),
            pltpu.VMEM((16, cap, 128), F32),
            pltpu.VMEM((16, cap, rows), BF16),
            pltpu.VMEM((16, rows, rows), BF16),
            pltpu.VMEM((4, 4, 16, rows), BF16),
            pltpu.VMEM((8, width), F32),
            pltpu.VMEM((4, 8, width), BF16),
            pltpu.VMEM((4, 3, 8, width), BF16),
            pltpu.VMEM((rows, width), BF16),
            pltpu.SemaphoreType.DMA((138,)),
            pltpu.SemaphoreType.DMA((138,)),
            pltpu.SemaphoreType.DMA((13,)),
        ],
        compiler_params=pltpu.CompilerParams(
            collective_id=1, has_side_effects=True, vmem_limit_bytes=67043328
        ),
        name="layer",
    )(
        prefill_rows,
        decode_rows,
        attended,
        decode_attended,
        feedforward_gain.reshape(1, width),
        out_projection,
        projection,
        routes.T,
        route_weight.T,
        decode_routes,
        decode_weight,
        shared_gate.reshape(1, width),
        expert_gate_up[0],
        expert_down[0],
        jnp.transpose(shared_gate_up, (1, 2, 0)),
        shared_down,
    )
    return pl.pallas_call(
        write_kernel,
        out_shape=tuple(jax.ShapeDtypeStruct(r.shape, r.dtype) for r in results),
        in_specs=[vmem, vmem],
        out_specs=(vmem, vmem),
        name="write",
    )(*results)


def solution(mesh):
    return jax.shard_map(
        per_device,
        mesh=mesh,
        in_specs=(
            P(("blk", "expert"), None),
            P(),
            P(None, None, "blk", "expert"),
            P(),
            P(),
            P(),
            P(None, None, "expert"),
            P("expert", None),
            P(("blk", "expert"), None),
            P(("blk", "expert"), None),
            P(),
            P(),
            P("expert", None, None),
            P("expert", None, None),
            P(None, None, "expert"),
            P("expert", None),
            P(),
        ),
        out_specs=(P(("blk", "expert"), None), P()),
        check_vma=False,
    )
```
